128 devices in a mesh: exp: 32 (over z_lo, x, y), strip: 4 (over z_hi, core).
Axes of the slice: x: 4, y: 4, z: 4 (z_hi: 2, z_lo: 2; z = z_hi * 2 + z_lo), core: 2. Of those that a mesh axis runs over, the one named last changes fastest.
Arguments:
- science: float32 [32, 512, 2048], P('exp', 'strip'), may hold values from -30 to 30
- variance: float32 [32, 512, 2048], P('exp', 'strip'), may hold values from 0.25 to 4
- template: float32 [576, 2176], P(None, 'exp'), may hold values from -14 to 14
- offset_rows: int32 [32], P('exp'), may hold values from 0 to 24
- offset_cols: int32 [32], P('exp'), may hold values from 0 to 88
- stamp_rows: int32 [32, 64], P('exp', 'strip'), may hold values from 0 to 96
- stamp_cols: int32 [32, 64], P('exp', 'strip'), may hold values from 0 to 2016
Outputs:
- difference: float32 [32, 512, 2048], P('exp', 'strip')
The draws below stay inside these ranges and needn't reach their ends.
All inputs are finite; a program needn't handle non-finite values.
Results may differ from the reference program's by a relative error of at most 0.0047.
Values sent between devices are 32-bit elements; how exact they have to be, the bound alone decides.
No kernel may reach another device: no remote copies, remote signals or barrier semaphores. Data moves between devices by JAX's collectives and lax.ppermute only.
A program may use at most 128 MiB of HBM per device.

```python
import jax
import jax.numpy as jnp
from jax import lax

STRIP_ROWS = 128
COLUMNS = 2048
STAMP_COUNT = 16
STAMP_SIZE = 32
BASES = 27
SPATIAL_TERMS = 6
BACKGROUND_TERMS = 3
SHIFT_MAX_ROWS = 24
KERNEL_HALF = 20
UNKNOWNS = 165
EXPOSURES = 32
IMAGE_ROWS = 512
STAMPS = 64
TEMPLATE_ROWS = 576
TEMPLATE_COLS = 2176
SHIFT_MAX_COLS = 88


def shift_draw(key, stream_id, largest):
    values = jax.random.randint(jax.random.fold_in(key, stream_id), (EXPOSURES,), 0, largest + 1)
    chosen = jax.random.randint(jax.random.fold_in(key, stream_id + 1), (), 0, EXPOSURES)
    second = (chosen + 1 + jax.random.randint(jax.random.fold_in(key, stream_id + 2), (), 0, EXPOSURES - 1)) % EXPOSURES
    places = jnp.arange(EXPOSURES)
    values = jnp.where(places == chosen, largest, values)
    values = jnp.where(places == second, 0, values)
    return values.astype(jnp.int32)


def template_draw(key):
    shape_all = (TEMPLATE_ROWS, TEMPLATE_COLS)
    scales = 2.0 * jnp.exp(jax.random.uniform(jax.random.fold_in(key, 3001), shape_all, jnp.float32, -0.5, 0.5))
    rough_part = jax.random.truncated_normal(jax.random.fold_in(key, 3003), -4.0, 4.0, shape_all, jnp.float32)
    return scales * rough_part


def variance_draw(key):
    shape_all = (EXPOSURES, IMAGE_ROWS, COLUMNS)
    return jnp.exp(jax.random.uniform(jax.random.fold_in(key, 5003), shape_all, jnp.float32, -1.3862944, 1.3862944))


def draw_template(key, part):
    return template_draw(key)


def draw_variance(key, part):
    return variance_draw(key)


def draw_offset_rows(key, part):
    return shift_draw(key, 1000, SHIFT_MAX_ROWS)


def draw_offset_cols(key, part):
    return shift_draw(key, 2000, SHIFT_MAX_COLS)


def draw_science(key, part):
    template = template_draw(key)
    variance = variance_draw(key)
    shift_down = shift_draw(key, 1000, SHIFT_MAX_ROWS)
    shift_side = shift_draw(key, 2000, SHIFT_MAX_COLS)
    kernel_grid = jnp.arange(3, dtype=jnp.float32) - 1.0
    radius = kernel_grid[:, None] ** 2 + kernel_grid[None, :] ** 2
    jitter = jax.random.normal(jax.random.fold_in(key, 4001), (EXPOSURES, 3, 3), jnp.float32)
    kernels = jnp.exp(-radius / 1.28)[None] * jnp.exp(0.4 * jitter)
    kernels = kernels / jnp.sum(kernels, axis=(1, 2), keepdims=True)
    tilt_terms = jax.random.uniform(jax.random.fold_in(key, 4002), (EXPOSURES, 2), jnp.float32, -0.3, 0.3)
    levels = jax.random.uniform(jax.random.fold_in(key, 4003), (EXPOSURES, 3), jnp.float32, -1.0, 1.0)
    shape_all = (EXPOSURES, IMAGE_ROWS, COLUMNS)
    noise_draw = jax.random.truncated_normal(jax.random.fold_in(key, 4005), -4.0, 4.0, shape_all, jnp.float32)
    side_pos = (2.0 * jnp.arange(COLUMNS, dtype=jnp.float32) + 1.0 - COLUMNS) / COLUMNS
    down_pos = (2.0 * jnp.arange(IMAGE_ROWS, dtype=jnp.float32) + 1.0 - IMAGE_ROWS) / IMAGE_ROWS

    def one_exposure(inputs):
        down_shift, side_shift, kernel, tilt_pair, level_terms, noise_var, noise_value = inputs
        window = lax.dynamic_slice(template, (down_shift + KERNEL_HALF - 1, side_shift + KERNEL_HALF - 1), (IMAGE_ROWS + 2, COLUMNS + 2))
        signal = jnp.zeros((IMAGE_ROWS, COLUMNS), jnp.float32)
        for i in range(3):
            for j in range(3):
                signal = signal + kernel[i, j] * window[i:i + IMAGE_ROWS, j:j + COLUMNS]
        signal = signal * (1.0 + tilt_pair[0] * side_pos[None, :] + tilt_pair[1] * down_pos[:, None])
        signal = signal + level_terms[0] + level_terms[1] * side_pos[None, :] + level_terms[2] * down_pos[:, None]
        return signal + jnp.sqrt(noise_var) * noise_value
    return lax.map(one_exposure, (shift_down, shift_side, kernels, tilt_terms, levels, variance, noise_draw))


def touch_ends(values, own_key, low, top_value):
    shape = values.shape
    index_at = [jax.random.randint(jax.random.fold_in(own_key, axis), (), 0, shape[axis]) for axis in range(len(shape))]
    values = values.at[tuple(index_at)].set(low)
    longest = shape.index(max(shape))
    index_at[longest] = (index_at[longest] + 1) % shape[longest]
    return values.at[tuple(index_at)].set(top_value)


def setup_inputs(seed: int = 0) -> dict:
    seeds = jax.random.split(jax.random.key(seed), 8)
    return {
        "science": draw_science(jax.random.fold_in(seeds[7], 71), 0),
        "variance": draw_variance(jax.random.fold_in(seeds[7], 71), 0),
        "template": draw_template(jax.random.fold_in(seeds[7], 71), 0),
        "offset_rows": draw_offset_rows(jax.random.fold_in(seeds[7], 71), 0),
        "offset_cols": draw_offset_cols(jax.random.fold_in(seeds[7], 71), 0),
        "stamp_rows": touch_ends(jax.random.randint(seeds[5], (EXPOSURES, STAMPS), 0, STRIP_ROWS - STAMP_SIZE + 1), jax.random.fold_in(seeds[5], 1), 0, STRIP_ROWS - STAMP_SIZE).astype(jnp.int32),
        "stamp_cols": touch_ends(jax.random.randint(seeds[6], (EXPOSURES, STAMPS), 0, COLUMNS - STAMP_SIZE + 1), jax.random.fold_in(seeds[6], 1), 0, COLUMNS - STAMP_SIZE).astype(jnp.int32),
    }


SIGMAS = (1.0, 2.0, 4.0)
DEGREES = (4, 2, 2)
RIDGE = 0.001

def filter_table(half_width):
    offsets = jnp.arange(-half_width, half_width + 1).astype(jnp.float32)
    entries = []
    for spread, degree in zip(SIGMAS, DEGREES):
        profile = jnp.exp(-offsets * offsets / (2.0 * spread * spread))
        profile = profile / jnp.sum(profile)
        scaled = offsets / spread
        for exponent in range(degree + 1):
            power = jnp.ones_like(scaled)
            for step in range(exponent):
                power = power * scaled
            entries.append(power * profile)
    return jnp.stack(entries)

def filter_groups():
    groups_list = []
    first_filter = 0
    basis_number = 0
    for degree in DEGREES:
        members_by = [[] for b in range(degree + 1)]
        for across in range(degree + 1):
            for downward in range(degree + 1 - across):
                members_by[downward].append((basis_number, first_filter + across))
                basis_number += 1
        for downward in range(degree + 1):
            groups_list.append((first_filter + downward, members_by[downward]))
        first_filter += degree + 1
    return groups_list

def band_matrix(tap_table, block_size):
    tap_count = tap_table.shape[1]
    distance = jnp.arange(block_size + tap_count - 1)[:, None] - jnp.arange(block_size)[None, :]
    onehot = (jnp.arange(tap_count)[:, None, None] == distance[None]).astype(jnp.float32)
    return jnp.einsum('ft,tjc->fjc', tap_table.astype(jnp.float32), onehot, precision=lax.Precision.HIGHEST)

def filter_down(picture, tap_table, out_rows):
    tap_count = tap_table.shape[1]
    block_size = min(128, out_rows)
    banded = band_matrix(tap_table, block_size)
    slab_stack = jnp.stack([picture[i * block_size:i * block_size + block_size + tap_count - 1] for i in range(out_rows // block_size)], 0)
    result = jnp.einsum('njc,fjr->fnrc', slab_stack.astype(jnp.float32), banded.astype(jnp.float32), precision=lax.Precision.HIGHEST, preferred_element_type=jnp.float32)
    return result.reshape(tap_table.shape[0], out_rows, picture.shape[1])

def filter_across(picture, tap_table, out_cols):
    tap_count = tap_table.shape[1]
    block_size = min(128, out_cols)
    banded = band_matrix(tap_table, block_size)
    slab_stack = jnp.stack([picture[..., i * block_size:i * block_size + block_size + tap_count - 1] for i in range(out_cols // block_size)], -2)
    result = jnp.einsum('...nj,fjc->f...nc', slab_stack.astype(jnp.float32), banded.astype(jnp.float32), precision=lax.Precision.HIGHEST, preferred_element_type=jnp.float32)
    return result.reshape(result.shape[:-2] + (out_cols,))

def spatial_terms(across, downward):
    all_ones = jnp.ones_like(across * downward)
    return [all_ones, across * all_ones, downward * all_ones, across * across * all_ones, across * downward, downward * downward * all_ones]

def ridge_solve(normal, right_side):
    unknowns = normal.shape[0]
    ridge_value = RIDGE * jnp.trace(normal) / unknowns
    factor = jnp.linalg.cholesky(normal + ridge_value * jnp.eye(unknowns, dtype=normal.dtype))
    middle = lax.linalg.triangular_solve(factor, right_side[:, None], left_side=True, lower=True)
    result = lax.linalg.triangular_solve(factor, middle, left_side=True, lower=True, transpose_a=True)
    return result[:, 0]

def stamp_design(vertical, picture, noise_var, top_rows, left_cols, row_base, image_rows, short_taps, groups_list):
    filters = vertical.shape[0]
    inside = jnp.arange(STAMP_SIZE)

    def cut_filtered(top_row, left_col):
        anchor = jnp.zeros((), jnp.int32)
        return lax.dynamic_slice(vertical, (anchor, top_row, left_col), (filters, STAMP_SIZE, STAMP_SIZE + 2 * KERNEL_HALF))

    def cut_plain(source, top_row, left_col):
        return lax.dynamic_slice(source, (top_row, left_col), (STAMP_SIZE, STAMP_SIZE))
    cutouts = jax.vmap(cut_filtered)(top_rows, left_cols)
    sci_stamps = jax.vmap(cut_plain, (None, 0, 0))(picture, top_rows, left_cols)
    var_stamps = jax.vmap(cut_plain, (None, 0, 0))(noise_var, top_rows, left_cols)
    basis_list = [None] * BASES
    for index_down, members in groups_list:
        filtered = filter_across(cutouts[:, index_down], short_taps[members[0][1]:members[-1][1] + 1], STAMP_SIZE)
        for position, member in enumerate(members):
            basis_list[member[0]] = filtered[position]
    pixel_rows = (row_base + top_rows[:, None, None] + inside[None, :, None]).astype(jnp.float32)
    pixel_cols = (left_cols[:, None, None] + inside[None, None, :]).astype(jnp.float32)
    across = (2.0 * pixel_cols + 1.0 - COLUMNS) / COLUMNS
    downward = (2.0 * pixel_rows + 1.0 - image_rows) / image_rows
    term_list = spatial_terms(across, downward)
    columns_list = []
    for basis_number in range(BASES):
        for spatial in term_list:
            columns_list.append(spatial * basis_list[basis_number])
    for spatial in term_list[:BACKGROUND_TERMS]:
        columns_list.append(spatial)
    design = jnp.stack(columns_list).reshape(UNKNOWNS, -1)
    weights = (1.0 / var_stamps).reshape(-1)
    weighted = design * weights[None, :]
    normal = jnp.dot(weighted.astype(jnp.float32), design.T.astype(jnp.float32), precision=lax.Precision.HIGHEST, preferred_element_type=jnp.float32)
    right_side = jnp.dot(weighted.astype(jnp.float32), sci_stamps.reshape(-1).astype(jnp.float32), precision=lax.Precision.HIGHEST, preferred_element_type=jnp.float32)
    return (normal, right_side)

def model_image(vertical_cols, coefficients, full_terms, short_taps, groups_list, out_cols):
    offset_bg = SPATIAL_TERMS * BASES
    predicted = coefficients[offset_bg] * full_terms[0]
    for i in range(1, BACKGROUND_TERMS):
        predicted = predicted + coefficients[offset_bg + i] * full_terms[i]
    for index_down, members in groups_list:
        filtered = filter_across(vertical_cols[index_down], short_taps[members[0][1]:members[-1][1] + 1], out_cols)
        for position, member in enumerate(members):
            basis_number = member[0]
            spatial_field = coefficients[SPATIAL_TERMS * basis_number] * full_terms[0]
            for j in range(1, SPATIAL_TERMS):
                spatial_field = spatial_field + coefficients[SPATIAL_TERMS * basis_number + j] * full_terms[j]
            predicted = predicted + spatial_field * filtered[position]
    return predicted

def reference(science, variance, template, offset_rows, offset_cols, stamp_rows, stamp_cols):
    tap_table = filter_table(KERNEL_HALF).astype(jnp.float32)
    short_taps = tap_table.astype(jnp.bfloat16)
    groups_list = filter_groups()
    column_pos = (2.0 * jnp.arange(COLUMNS, dtype=jnp.float32) + 1.0 - COLUMNS) / COLUMNS
    row_pos = (2.0 * jnp.arange(IMAGE_ROWS, dtype=jnp.float32) + 1.0 - IMAGE_ROWS) / IMAGE_ROWS
    full_terms = spatial_terms(column_pos[None, :], row_pos[:, None])
    strip_start = (jnp.arange(STAMPS) // STAMP_COUNT * STRIP_ROWS).astype(jnp.int32)

    def one_exposure(inputs):
        picture, noise_var, shift_down, shift_side, corner_down, corner_side = inputs
        window = lax.dynamic_slice(template, (shift_down.astype(jnp.int32), shift_side.astype(jnp.int32)), (IMAGE_ROWS + 2 * KERNEL_HALF, COLUMNS + 2 * KERNEL_HALF))
        vertical = filter_down(window, tap_table, IMAGE_ROWS).astype(jnp.bfloat16)
        top_rows = (strip_start + corner_down.astype(jnp.int32)).astype(jnp.int32)
        left_cols = corner_side.astype(jnp.int32)
        normal, right_side = stamp_design(vertical, picture, noise_var, top_rows, left_cols, jnp.zeros((), jnp.int32), IMAGE_ROWS, short_taps, groups_list)
        coefficients = ridge_solve(normal, right_side)
        predicted = model_image(vertical, coefficients, full_terms, short_taps, groups_list, COLUMNS)
        return picture - predicted
    return lax.map(one_exposure, (science, variance, offset_rows, offset_cols, stamp_rows, stamp_cols))
```

```python
import functools
import math

import jax
import jax.numpy as jnp
import ml_dtypes
import numpy as np
from jax import lax
from jax.experimental import pallas as pl
from jax.experimental.pallas import tpu as pltpu
from jax.sharding import PartitionSpec as P

STRIP_ROWS = 128
COLUMNS = 2048
IMAGE_ROWS = 512
STAMP_COUNT = 16
STAMP_SIZE = 32
SPATIAL_TERMS = 6
KERNEL_HALF = 20
UNKNOWNS = 165
RIDGE = 0.001
SIGMAS = (1.0, 2.0, 4.0)
DEGREES = (4, 2, 2)

LANES = 128
SOURCE_COLS = 68
NEED_ROWS = 192
WIDE = 2176
PATCH = 80
WINDOW = 176
CUT_ROWS = 40
PIECE_A = 56
PIECE_B = 48

G0, G1, G2 = 0, 5, 8
TILES = (
    ((G0 + 0, (0, 1, 2, 3, 4)), (G0 + 2, (0, 1, 2))),
    ((G0 + 1, (0, 1, 2, 3)), (G0 + 3, (0, 1)), (G0 + 4, (0,))),
    ((G1 + 0, (5, 6, 7)), (G1 + 1, (5, 6)), (G1 + 2, (5,))),
    ((G2 + 0, (8, 9, 10)), (G2 + 1, (8, 9)), (G2 + 2, (8,))),
)
CONST_SLOT = 15
SCIENCE_SLOT = 22
SLOTS = 32
PADDED = SPATIAL_TERMS * SLOTS


def tap_table():
    offsets = np.arange(-KERNEL_HALF, KERNEL_HALF + 1).astype(np.float64)
    entries = []
    for spread, degree in zip(SIGMAS, DEGREES):
        profile = np.exp(-offsets * offsets / (2.0 * spread * spread))
        profile = profile / profile.sum()
        for exponent in range(degree + 1):
            entries.append((offsets / spread) ** exponent * profile)
    table = np.stack(entries)
    table[np.abs(table) < 1.2e-38] = 0.0
    return table.astype(np.float32)


def split_halves(table):
    high = table.astype(ml_dtypes.bfloat16)
    low = (table - high.astype(np.float32)).astype(ml_dtypes.bfloat16)
    return high, low


def down_rows(filters, rows):
    taps = tap_table()
    full = np.zeros((len(filters), rows, PATCH), np.float32)
    for i, f in enumerate(filters):
        if f is not None:
            for r in range(rows):
                full[i, r, r : r + 2 * KERNEL_HALF + 1] = taps[f]
    high, low = split_halves(full)
    return np.concatenate([high, high, low], axis=2)


def stamp_down():
    blocks = []
    for tile in TILES:
        filters = [f for _, down in tile for f in down]
        filters += [None] * (8 - len(filters))
        blocks.append(down_rows(filters, STAMP_SIZE).transpose(1, 0, 2).reshape(-1, 3 * PATCH))
    return np.concatenate(blocks)


def full_down():
    return down_rows(list(range(11)), STAMP_SIZE).reshape(-1, 3 * PATCH)


def across_band(width):
    short = tap_table().astype(ml_dtypes.bfloat16)
    band = np.zeros((2 * LANES, 11, width), ml_dtypes.bfloat16)
    for m in range(11):
        for c in range(width):
            band[c : c + 2 * KERNEL_HALF + 1, m, c] = short[m]
    return band


def stamp_across(tile):
    band = across_band(STAMP_SIZE)[:LANES]
    out = np.zeros((4, LANES, len(tile), 4, STAMP_SIZE), ml_dtypes.bfloat16)
    for i, (m, _) in enumerate(tile):
        for s in range(4):
            out[s, :, i, s, :] = band[:, m]
    return out.reshape(4 * LANES, len(tile) * LANES)


def slot_of():
    slots = []
    for t, tile in enumerate(TILES):
        s = 8 * t
        for across, down in tile:
            for f in down:
                slots.append((s, f, across))
                s += 1
    return slots


def pack_kernel(strip_ref, template_ref, a_ref, b_ref):
    start = pl.multiple_of(strip_ref[0] * LANES, LANES)
    first = template_ref[:, pl.ds(start, LANES)]
    second = template_ref[:, pl.ds(start + LANES, NEED_ROWS - LANES)]
    half = SOURCE_COLS // 2
    a_ref[...] = first[:PIECE_A]
    b_ref[...] = jnp.zeros_like(b_ref)
    b_ref[0:half, 0:64] = second[:half]
    b_ref[0:half, 64:128] = second[half:]
    b_ref[half : half + SOURCE_COLS - PIECE_A, :] = first[PIECE_A:]


def stamps_kernel(scalars, rows_ref, cols_ref, *refs):
    a_refs = refs[0:4]
    b_refs = refs[4:8]
    science_ref, variance_ref, down_ref = refs[8:11]
    across_refs = refs[11:15]
    gram_ref, window_ref = refs[15:17]
    t_one, t_two, w_buf, patches, vert, cut_buf, sci_buf, wt_buf, bases, design = refs[17:]
    place, shift_down, shift_side, row_base = scalars[0], scalars[1], scalars[2], scalars[3]
    my_z, my_x, my_y = place // 16, (place // 4) % 4, place % 4
    half = SOURCE_COLS // 2
    offsets = (0, 3, 1, 2)
    for first in range(4):
        for second in range(4):
            for dz in range(2):
                for is_a in (True, False):
                    along_x, along_y = (first, second) if is_a else (second, first)
                    source = (
                        ((my_z + dz) % 2) * 16
                        + ((my_x + offsets[along_x]) % 4) * 4
                        + (my_y + offsets[along_y]) % 4
                    )
                    base = source * SOURCE_COLS
                    if is_a:
                        t_one[pl.ds(base, PIECE_A), :] = a_refs[first][second, dz]
                    else:
                        rest = b_refs[first][second, dz, 0:half, :]
                        t_two[pl.ds(base, half), :] = rest
                        t_two[pl.ds(base + half, half), :] = pltpu.roll(rest, 64, 1)
                        t_one[pl.ds(base + PIECE_A, SOURCE_COLS - PIECE_A), :] = b_refs[first][
                            second, dz, half : half + SOURCE_COLS - PIECE_A, :
                        ]
    t_one[pl.ds(WIDE, LANES), :] = jnp.zeros((LANES, LANES), jnp.float32)
    t_two[pl.ds(WIDE, LANES), :] = jnp.zeros((LANES, LANES), jnp.float32)
    w_buf[:, NEED_ROWS:, :] = jnp.zeros((WIDE // LANES, 8, LANES), jnp.float32)

    @pl.loop(0, WIDE // LANES)
    def _(i):
        w_buf[i, 0:LANES, :] = t_one[pl.ds(shift_side + i * LANES, LANES), :].T
        w_buf[i, LANES:NEED_ROWS, :] = t_two[pl.ds(shift_side + i * LANES, LANES), :].T[
            0 : NEED_ROWS - LANES
        ]
        window_ref[i, :, :] = w_buf[i, pl.ds(shift_down, WINDOW), :]

    lane = lax.broadcasted_iota(jnp.int32, (1, LANES), 1)

    @pl.loop(0, STAMP_COUNT)
    def _(s):
        top, left = rows_ref[s], cols_ref[s]
        tile = left // LANES
        rest = left % LANES
        back = (LANES - rest) % LANES
        low = pltpu.roll(window_ref[tile, pl.ds(top, PATCH), :], back, 1)
        high = pltpu.roll(window_ref[tile + 1, pl.ds(top, PATCH), :], back, 1)
        patch = jnp.where(lane < LANES - rest, low, high)
        patch_high = patch.astype(jnp.bfloat16)
        patch_low = (patch - patch_high.astype(jnp.float32)).astype(jnp.bfloat16)
        here = pl.ds(pl.multiple_of(s * LANES, LANES), LANES)
        patches[0:PATCH, here] = patch_high
        patches[PATCH : 2 * PATCH, here] = patch_low
        patches[2 * PATCH :, here] = patch_high

    slot = lax.broadcasted_iota(jnp.int32, (8, LANES), 0)

    @pl.loop(0, STAMP_COUNT // 4)
    def _(group):
        science = jnp.zeros((STAMP_SIZE, LANES), jnp.float32)
        noise = jnp.ones((STAMP_SIZE, LANES), jnp.float32)
        x_row = jnp.zeros((1, LANES), jnp.float32)
        y_row = jnp.zeros((1, LANES), jnp.float32)
        for member in range(4):
            s = 4 * group + member
            top, left = rows_ref[s], cols_ref[s]
            tile = left // LANES
            tile_start = pl.multiple_of(tile * LANES, LANES)
            next_start = pl.multiple_of(jnp.minimum(tile + 1, COLUMNS // LANES - 1) * LANES, LANES)
            rest = left % LANES
            turn = (LANES + STAMP_SIZE * member - rest) % LANES
            inside = (lane >= STAMP_SIZE * member) & (lane < STAMP_SIZE * (member + 1))
            from_low = lane - STAMP_SIZE * member + rest < LANES
            row_start = pl.multiple_of(jnp.minimum((top // 8) * 8, STRIP_ROWS - CUT_ROWS), 8)
            row_rest = top - row_start
            pieces = []
            for n, ref in enumerate((science_ref, variance_ref)):
                low = pltpu.roll(ref[pl.ds(row_start, CUT_ROWS), pl.ds(tile_start, LANES)], turn, 1)
                high = pltpu.roll(ref[pl.ds(row_start, CUT_ROWS), pl.ds(next_start, LANES)], turn, 1)
                cut_buf[member, n, :, :] = jnp.where(from_low, low, high)
                pieces.append(cut_buf[member, n, pl.ds(row_rest, STAMP_SIZE), :])
            science = jnp.where(inside, pieces[0], science)
            noise = jnp.where(inside, pieces[1], noise)
            col = (left + lane - STAMP_SIZE * member).astype(jnp.float32)
            row = (row_base + top + jnp.zeros_like(lane)).astype(jnp.float32)
            x_row = jnp.where(inside, (2.0 * col + 1.0 - COLUMNS) / COLUMNS, x_row)
            y_row = jnp.where(inside, (2.0 * row + 1.0 - IMAGE_ROWS) / IMAGE_ROWS, y_row)
        sci_buf[...] = science
        wt_buf[...] = lax.rsqrt(noise)
        x = jnp.broadcast_to(x_row, (8, LANES))
        y_first = jnp.broadcast_to(y_row, (8, LANES))
        vert[...] = jnp.dot(
            down_ref[...],
            patches[:, pl.ds(pl.multiple_of(group * 4 * LANES, 4 * LANES), 4 * LANES)],
            preferred_element_type=jnp.float32,
        ).astype(jnp.bfloat16)
        for t, tile in enumerate(TILES):
            out = jnp.dot(
                vert[t * 256 : (t + 1) * 256, :], across_refs[t][...], preferred_element_type=jnp.float32
            )
            out = out.reshape(STAMP_SIZE, 8, len(tile) * LANES)
            value = out[:, :, 0:LANES]
            edge = len(tile[0][1])
            for i in range(1, len(tile)):
                value = jnp.where(slot[None] >= edge, out[:, :, i * LANES : (i + 1) * LANES], value)
                edge += len(tile[i][1])
            if t == CONST_SLOT // 8:
                value = jnp.where(slot[None] == CONST_SLOT % 8, 1.0, value)
            bases[t, :, :, :] = value

        @pl.loop(0, STAMP_SIZE // 4)
        def _(quarter):
            for inner in range(4):
                r = quarter * 4 + inner
                science = jnp.broadcast_to(sci_buf[pl.ds(r, 1), :], (8, LANES))
                weight = jnp.broadcast_to(wt_buf[pl.ds(r, 1), :], (8, LANES))
                tiles = [bases[t, r] for t in range(4)]
                tiles[SCIENCE_SLOT // 8] = jnp.where(
                    slot == SCIENCE_SLOT % 8, science, tiles[SCIENCE_SLOT // 8]
                )
                y = y_first + (2.0 / IMAGE_ROWS) * r.astype(jnp.float32)
                tiles = [b * weight for b in tiles]
                terms = (None, x, y, x * x, x * y, y * y)
                start = pl.multiple_of((group * STAMP_SIZE + r) * LANES, LANES)
                for j, term in enumerate(terms):
                    values = tiles if term is None else [b * term for b in tiles]
                    design[j * SLOTS : (j + 1) * SLOTS, pl.ds(start, LANES)] = jnp.concatenate(
                        values, axis=0
                    ).astype(jnp.bfloat16)

    gram_ref[...] = jnp.zeros_like(gram_ref)

    @pl.loop(0, 16)
    def _(chunk):
        part = design[:, pl.ds(pl.multiple_of(chunk * 1024, 1024), 1024)]
        gram_ref[...] += lax.dot_general(
            part, part, (((1,), (1,)), ((), ())), preferred_element_type=jnp.float32
        )


def down_kernel(down_ref, window_ref, out_ref):
    for block in range(STRIP_ROWS // STAMP_SIZE):
        piece = window_ref[0, block * STAMP_SIZE : block * STAMP_SIZE + PATCH, :]
        high = piece.astype(jnp.bfloat16)
        low = (piece - high.astype(jnp.float32)).astype(jnp.bfloat16)
        stacked = jnp.concatenate([high, low, high], axis=0)
        out = jnp.dot(down_ref[...], stacked, preferred_element_type=jnp.float32)
        out_ref[:, block * STAMP_SIZE : (block + 1) * STAMP_SIZE, :] = out.astype(jnp.bfloat16).reshape(
            11, STAMP_SIZE, LANES
        )


def lane_spread(value, index):
    return jnp.broadcast_to(value[:, index : index + 1], (8, LANES))


def solve(gram_ref):
    row_id = lax.broadcasted_iota(jnp.int32, (8, LANES), 0)
    lane_id = lax.broadcasted_iota(jnp.int32, (8, LANES), 1)
    slots = sorted(s for s, _, _ in slot_of())
    pivots = sorted(slots + [CONST_SLOT])
    active = {32 * j + s for j in range(SPATIAL_TERMS) for s in slots}
    active |= {32 * j + CONST_SLOT for j in range(3)}

    def any_of(ids, chosen):
        mask = jnp.zeros(ids.shape, jnp.bool_)
        for c in chosen:
            mask = mask | (ids == c)
        return mask

    lanes_left = any_of(lane_id, sorted(u for u in active if u < LANES) + [SCIENCE_SLOT])
    lanes_right = any_of(lane_id, [u - LANES for u in sorted(active) if u >= LANES])
    left, right = [], []
    total = jnp.zeros((8, LANES), jnp.float32)
    pad = jnp.zeros((8, 2 * LANES - PADDED), jnp.float32)
    diagonals = []
    for i in range(24):
        rows = any_of(row_id, [u - 8 * i for u in sorted(active) if u // 8 == i])
        a = jnp.where(rows & lanes_left, gram_ref[8 * i : 8 * i + 8, 0:LANES], 0.0)
        b = jnp.concatenate([gram_ref[8 * i : 8 * i + 8, LANES:PADDED], pad], axis=1)
        b = jnp.where(rows & lanes_right, b, 0.0)
        diagonal = lane_id == (row_id + 8 * i) % LANES
        total = total + jnp.where(diagonal & rows, a if i < 16 else b, 0.0)
        left.append(a)
        right.append(b)
        diagonals.append((diagonal, rows))
    ridge = jnp.sum(total, axis=(0, 1), keepdims=True) * (RIDGE / UNKNOWNS)
    for i, (diagonal, rows) in enumerate(diagonals):
        added = jnp.where(diagonal, jnp.where(rows, ridge, 1.0), 0.0)
        if i < 16:
            left[i] = left[i] + jnp.where(lane_id == SCIENCE_SLOT, 0.0, added)
        else:
            right[i] = right[i] + added

    def eliminate(left, right, high):
        left, right = list(left), list(right)
        for p in pivots:
            tile, sub = p // 8, p % 8
            source = right if high else left
            pivot_row = jnp.broadcast_to(source[tile][sub : sub + 1, :], (8, LANES))
            spread = 1.0 / lane_spread(pivot_row, p)
            left_row = jnp.broadcast_to(left[tile][sub : sub + 1, :], (8, LANES)) * spread
            right_row = pivot_row * spread if high else None
            for i in range(24):
                factor = lane_spread(source[i], p)
                value = left[i] - factor * left_row
                left[i] = jnp.where(row_id == sub, left_row, value) if i == tile else value
                if high:
                    value = right[i] - factor * right_row
                    right[i] = jnp.where(row_id == sub, right_row, value) if i == tile else value
        left = left[4:] + left[:4]
        if high:
            right = [pltpu.roll(v, LANES - SLOTS, 1) for v in right[4:] + right[:4]]
        else:
            left = [pltpu.roll(v, LANES - SLOTS, 1) for v in left]
        return tuple(left), tuple(right)

    left, right = left[16:] + left[:16], right[16:] + right[:16]
    left, right = lax.fori_loop(0, 2, lambda _, c: eliminate(c[0], c[1], True), (tuple(left), tuple(right)))
    left = lax.fori_loop(0, 4, lambda _, c: eliminate(c, (), False)[0], left)
    left = left[8:] + left[:8]
    return [lane_spread(v, SCIENCE_SLOT) for v in left]


def model_kernel(row_ref, gram_ref, vert_ref, science_ref, *refs):
    across_refs = refs[0:3]
    out_ref = refs[3]
    a_buf, b_buf, c_buf, basis = refs[4:8]
    solution_tiles = solve(gram_ref)
    lane_id = lax.broadcasted_iota(jnp.int32, (8, LANES), 1)
    row_id = lax.broadcasted_iota(jnp.int32, (8, LANES), 0)
    for i in range(COLUMNS // LANES):
        x = (2.0 * (lane_id + i * LANES).astype(jnp.float32) + 1.0 - COLUMNS) / COLUMNS
        for t in range(4):
            c = [solution_tiles[4 * j + t] for j in range(SPATIAL_TERMS)]
            here = slice(i * LANES, (i + 1) * LANES)
            a_buf[8 * t : 8 * t + 8, here] = c[0] + x * (c[1] + x * c[3])
            b_buf[8 * t : 8 * t + 8, here] = c[2] + x * c[4]
            if i == 0:
                c_buf[8 * t : 8 * t + 8, :] = c[5]
    base = row_ref[0]
    slots = slot_of()
    group_first = (G0, G1, G2)

    @pl.loop(0, COLUMNS // LANES)
    def _(i):
        start = pl.multiple_of(i * LANES, LANES)
        at = pl.ds(start, LANES)
        wide = pl.ds(start, 2 * LANES)
        for f in range(11):
            g = 0 if f < 5 else (1 if f < 8 else 2)
            members = [(s, m) for s, ff, m in slots if ff == f]
            out = jnp.dot(
                vert_ref[f, :, wide],
                across_refs[g][:, 0 : len(members) * LANES],
                preferred_element_type=jnp.float32,
            )
            for s, m in members:
                k = m - group_first[g]
                basis[s, :, :] = out[:, k * LANES : (k + 1) * LANES]

        @pl.loop(0, STRIP_ROWS // 8)
        def _(q):
            rows = pl.ds(pl.multiple_of(8 * q, 8), 8)
            y = (2.0 * (row_id + 8 * q + base).astype(jnp.float32) + 1.0 - IMAGE_ROWS) / IMAGE_ROWS
            zero = jnp.broadcast_to(a_buf[CONST_SLOT : CONST_SLOT + 1, at], (8, LANES))
            one = jnp.broadcast_to(b_buf[CONST_SLOT : CONST_SLOT + 1, at], (8, LANES))
            two = jnp.zeros((8, LANES), jnp.float32)
            for s, _, _ in slots:
                value = basis[s, rows, :]
                zero = zero + value * a_buf[s : s + 1, at]
                one = one + value * b_buf[s : s + 1, at]
                two = two + value * c_buf[s : s + 1, :]
            out_ref[rows, at] = science_ref[rows, at] - (zero + y * (one + y * two))


def exp_steps():
    def place(z, x, y):
        return (z % 2) * 16 + (x % 4) * 4 + y % 4

    def shift(dz, dx, dy):
        return [(place(z, x, y), place(z + dz, x + dx, y + dy)) for z in range(2) for x in range(4) for y in range(4)]

    return shift


def gather_template(piece_a, piece_b):
    shift = exp_steps()

    def move(value, *step):
        return lax.ppermute(value, "exp", shift(*step))

    along_x = ((0, 1, 0), (0, -1, 0), (0, 2, 0))
    along_y = ((0, 0, 1), (0, 0, -1), (0, 0, 2))
    piece = jnp.concatenate([piece_a, piece_b], axis=0)
    other = move(piece, 1, 0, 0)
    both = jnp.stack([piece, other])
    part_a, part_b = both[:, :PIECE_A], both[:, PIECE_A:]
    part_a = jnp.stack([part_a] + [move(part_a, *s) for s in along_y])
    part_b = jnp.stack([part_b] + [move(part_b, *s) for s in along_x])
    parts_a = [part_a] + [move(part_a, *s) for s in along_x]
    parts_b = [part_b] + [move(part_b, *s) for s in along_y]
    return parts_a, parts_b


def reduce_strips(value):
    value = value + lax.ppermute(value, "strip", [(0, 1), (1, 0), (2, 3), (3, 2)])
    return value + lax.ppermute(value, "strip", [(0, 2), (2, 0), (1, 3), (3, 1)])


VMEM = pltpu.MemorySpace.VMEM
SMEM = pltpu.MemorySpace.SMEM


def vmem():
    return pl.BlockSpec(memory_space=VMEM)


def smem():
    return pl.BlockSpec(memory_space=SMEM)


def shards(science, variance, template, offset_rows, offset_cols, stamp_rows, stamp_cols):
    strip_index = lax.axis_index("strip")
    place = lax.axis_index("exp")
    row_base = (strip_index * STRIP_ROWS).astype(jnp.int32)
    piece_a, piece_b = pl.pallas_call(
        pack_kernel,
        out_shape=(
            jax.ShapeDtypeStruct((PIECE_A, LANES), jnp.float32),
            jax.ShapeDtypeStruct((PIECE_B, LANES), jnp.float32),
        ),
        in_specs=[smem(), vmem()],
        out_specs=(vmem(), vmem()),
        name="pack",
    )(strip_index.astype(jnp.int32)[None], template.T)
    parts_a, parts_b = gather_template(piece_a, piece_b)
    scalars = jnp.stack([place.astype(jnp.int32), offset_rows[0], offset_cols[0], row_base])
    gram, window = pl.pallas_call(
        stamps_kernel,
        out_shape=(
            jax.ShapeDtypeStruct((PADDED, PADDED), jnp.float32),
            jax.ShapeDtypeStruct((WIDE // LANES, WINDOW, LANES), jnp.float32),
        ),
        in_specs=[smem()] * 3 + [vmem()] * 15,
        out_specs=(vmem(), vmem()),
        scratch_shapes=[
            pltpu.VMEM((WIDE + LANES, LANES), jnp.float32),
            pltpu.VMEM((WIDE + LANES, LANES), jnp.float32),
            pltpu.VMEM((WIDE // LANES, NEED_ROWS + 8, LANES), jnp.float32),
            pltpu.VMEM((3 * PATCH, STAMP_COUNT * LANES), jnp.bfloat16),
            pltpu.VMEM((1024, 4 * LANES), jnp.bfloat16),
            pltpu.VMEM((4, 2, CUT_ROWS, LANES), jnp.float32),
            pltpu.VMEM((STAMP_SIZE, LANES), jnp.float32),
            pltpu.VMEM((STAMP_SIZE, LANES), jnp.float32),
            pltpu.VMEM((4, STAMP_SIZE, 8, LANES), jnp.float32),
            pltpu.VMEM((PADDED, STAMP_COUNT * STAMP_SIZE * STAMP_SIZE), jnp.bfloat16),
        ],
        name="stamps",
    )(
        scalars,
        stamp_rows[0],
        stamp_cols[0],
        *parts_a,
        *parts_b,
        science[0],
        variance[0],
        jnp.asarray(stamp_down()),
        *[jnp.asarray(stamp_across(tile)) for tile in TILES],
    )
    vertical = pl.pallas_call(
        down_kernel,
        out_shape=jax.ShapeDtypeStruct((11, STRIP_ROWS, WIDE), jnp.bfloat16),
        grid=(WIDE // LANES,),
        in_specs=[
            pl.BlockSpec((11 * STAMP_SIZE, 3 * PATCH), lambda i: (0, 0)),
            pl.BlockSpec((1, WINDOW, LANES), lambda i: (i, 0, 0)),
        ],
        out_specs=pl.BlockSpec((11, STRIP_ROWS, LANES), lambda i: (0, 0, i)),
        cost_estimate=pl.CostEstimate(flops=int(4e9), bytes_accessed=int(8e6), transcendentals=0),
        name="down",
    )(jnp.asarray(full_down()), window)
    total = reduce_strips(gram)
    band = across_band(LANES)
    bands = [
        jnp.asarray(band[:, first : first + degree + 1].reshape(2 * LANES, -1))
        for first, degree in zip((G0, G1, G2), DEGREES)
    ]
    result = pl.pallas_call(
        model_kernel,
        out_shape=jax.ShapeDtypeStruct((STRIP_ROWS, COLUMNS), jnp.float32),
        in_specs=[smem()] + [vmem()] * 6,
        out_specs=vmem(),
        scratch_shapes=[
            pltpu.VMEM((SLOTS, COLUMNS), jnp.float32),
            pltpu.VMEM((SLOTS, COLUMNS), jnp.float32),
            pltpu.VMEM((SLOTS, LANES), jnp.float32),
            pltpu.VMEM((SLOTS, STRIP_ROWS, LANES), jnp.float32),
        ],
        name="model",
    )(row_base[None], total, vertical, science[0], *bands)
    return result[None]


def solution(mesh):
    in_specs = (
        P("exp", "strip", None),
        P("exp", "strip", None),
        P(None, "exp"),
        P("exp"),
        P("exp"),
        P("exp", "strip"),
        P("exp", "strip"),
    )
    out_specs = P("exp", "strip", None)
    return jax.shard_map(shards, mesh=mesh, in_specs=in_specs, out_specs=out_specs, check_vma=False)
```

```python
import itertools

import jax
import jax.numpy as jnp
import ml_dtypes
import numpy as np
from jax import lax
from jax.experimental import pallas as pl
from jax.experimental.pallas import tpu as pltpu
from jax.sharding import PartitionSpec as P

STRIP_ROWS = 128
COLUMNS = 2048
IMAGE_ROWS = 512
STAMP_COUNT = 16
STAMP_SIZE = 32
SPATIAL_TERMS = 6
KERNEL_HALF = 20
UNKNOWNS = 165
RIDGE = 0.001
SIGMAS = (1.0, 2.0, 4.0)
DEGREES = (4, 2, 2)

LANES = 128
SOURCE_COLS = 68
NEED_ROWS = 192
WIDE = 2176
TILE_COUNT = 18
PATCH = 80
WINDOW = 176
CUT_ROWS = 40
PIECE_A = 56
PIECE_B = 48

G0, G1, G2 = 0, 5, 8
TILES = (
    ((G0 + 0, (0, 1, 2, 3, 4)), (G0 + 2, (0, 1, 2))),
    ((G0 + 1, (0, 1, 2, 3)), (G0 + 3, (0, 1)), (G0 + 4, (0,))),
    ((G1 + 0, (5, 6, 7)), (G1 + 1, (5, 6)), (G1 + 2, (5,))),
    ((G2 + 0, (8, 9, 10)), (G2 + 1, (8, 9)), (G2 + 2, (8,))),
)
CONST_SLOT = 15
SCIENCE_SLOT = 22
SLOTS = 32
PADDED = SPATIAL_TERMS * SLOTS


def tap_table():
    offsets = np.arange(-KERNEL_HALF, KERNEL_HALF + 1).astype(np.float64)
    entries = []
    for spread, degree in zip(SIGMAS, DEGREES):
        profile = np.exp(-offsets * offsets / (2.0 * spread * spread))
        profile = profile / profile.sum()
        for exponent in range(degree + 1):
            entries.append((offsets / spread) ** exponent * profile)
    table = np.stack(entries)
    table[np.abs(table) < 1.2e-38] = 0.0
    return table.astype(np.float32)


def split_halves(table):
    high = table.astype(ml_dtypes.bfloat16)
    low = (table - high.astype(np.float32)).astype(ml_dtypes.bfloat16)
    return high, low


def down_rows(filters, rows):
    taps = tap_table()
    full = np.zeros((len(filters), rows, PATCH), np.float32)
    for i, f in enumerate(filters):
        if f is not None:
            for r in range(rows):
                full[i, r, r : r + 2 * KERNEL_HALF + 1] = taps[f]
    high, low = split_halves(full)
    return np.concatenate([high, high, low], axis=2)


def stamp_down():
    blocks = []
    for tile in TILES:
        filters = [f for _, down in tile for f in down]
        filters += [None] * (8 - len(filters))
        blocks.append(down_rows(filters, STAMP_SIZE).transpose(1, 0, 2).reshape(-1, 3 * PATCH))
    return np.concatenate(blocks)


def full_down():
    return down_rows(list(range(11)), STAMP_SIZE).reshape(-1, 3 * PATCH)


def across_band(width):
    short = tap_table().astype(ml_dtypes.bfloat16)
    band = np.zeros((2 * LANES, 11, width), ml_dtypes.bfloat16)
    for m in range(11):
        for c in range(width):
            band[c : c + 2 * KERNEL_HALF + 1, m, c] = short[m]
    return band


def stamp_across(tile):
    band = across_band(STAMP_SIZE)[:LANES]
    out = np.zeros((4, LANES, len(tile), 4, STAMP_SIZE), ml_dtypes.bfloat16)
    for i, (m, _) in enumerate(tile):
        for s in range(4):
            out[s, :, i, s, :] = band[:, m]
    return out.reshape(4 * LANES, len(tile) * LANES)


def slot_of():
    slots = []
    for t, tile in enumerate(TILES):
        s = 8 * t
        for across, down in tile:
            for f in down:
                slots.append((s, f, across))
                s += 1
    return slots


def pack_kernel(strip_ref, template_ref, a_ref, b_ref):
    start = pl.multiple_of(strip_ref[0] * LANES, LANES)
    first = template_ref[:, pl.ds(start, LANES)]
    second = template_ref[:, pl.ds(start + LANES, NEED_ROWS - LANES)]
    half = SOURCE_COLS // 2
    a_ref[...] = first[:PIECE_A]
    b_ref[...] = jnp.zeros_like(b_ref)
    b_ref[0:half, 0:64] = second[:half]
    b_ref[0:half, 64:128] = second[half:]
    b_ref[half : half + SOURCE_COLS - PIECE_A, :] = first[PIECE_A:]


def stamps_kernel(scalars, rows_ref, cols_ref, *refs):
    a_refs = refs[0:4]
    b_refs = refs[4:8]
    science_ref, variance_ref, down_ref = refs[8:11]
    across_refs = refs[11:15]
    gram_ref, window_ref = refs[15:17]
    t_one, t_two, w_buf, patches, vert, cut_buf, sci_buf, wt_buf, bases, design = refs[17:]
    place, shift_down, shift_side, row_base = scalars[0], scalars[1], scalars[2], scalars[3]
    my_z, my_x, my_y = place // 16, (place // 4) % 4, place % 4
    half = SOURCE_COLS // 2
    offsets = (0, 3, 1, 2)
    for first in range(4):
        for second in range(4):
            for dz in range(2):
                for is_a in (True, False):
                    along_x, along_y = (first, second) if is_a else (second, first)
                    source = (
                        ((my_z + dz) % 2) * 16
                        + ((my_x + offsets[along_x]) % 4) * 4
                        + (my_y + offsets[along_y]) % 4
                    )
                    base = source * SOURCE_COLS
                    if is_a:
                        t_one[pl.ds(base, PIECE_A), :] = a_refs[first][second, dz]
                    else:
                        rest = b_refs[first][second, dz, 0:half, :]
                        t_two[pl.ds(base, half), :] = rest
                        t_two[pl.ds(base + half, half), :] = pltpu.roll(rest, 64, 1)
                        t_one[pl.ds(base + PIECE_A, SOURCE_COLS - PIECE_A), :] = b_refs[first][
                            second, dz, half : half + SOURCE_COLS - PIECE_A, :
                        ]
    t_one[pl.ds(WIDE, 2 * LANES), :] = jnp.zeros((2 * LANES, LANES), jnp.float32)
    t_two[pl.ds(WIDE, 2 * LANES), :] = jnp.zeros((2 * LANES, LANES), jnp.float32)
    w_buf[:, NEED_ROWS:, :] = jnp.zeros((TILE_COUNT, 8, LANES), jnp.float32)

    @pl.loop(0, TILE_COUNT)
    def _(i):
        w_buf[i, 0:LANES, :] = t_one[pl.ds(shift_side + i * LANES, LANES), :].T
        w_buf[i, LANES:NEED_ROWS, :] = t_two[pl.ds(shift_side + i * LANES, LANES), :].T[
            0 : NEED_ROWS - LANES
        ]
        window_ref[i, :, :] = w_buf[i, pl.ds(shift_down, WINDOW), :]

    lane = lax.broadcasted_iota(jnp.int32, (1, LANES), 1)

    @pl.loop(0, STAMP_COUNT)
    def _(s):
        top, left = rows_ref[s], cols_ref[s]
        tile = left // LANES
        rest = left % LANES
        back = (LANES - rest) % LANES
        low = pltpu.roll(window_ref[tile, pl.ds(top, PATCH), :], back, 1)
        high = pltpu.roll(window_ref[tile + 1, pl.ds(top, PATCH), :], back, 1)
        patch = jnp.where(lane < LANES - rest, low, high)
        patch_high = patch.astype(jnp.bfloat16)
        patch_low = (patch - patch_high.astype(jnp.float32)).astype(jnp.bfloat16)
        here = pl.ds(pl.multiple_of(s * LANES, LANES), LANES)
        patches[0:PATCH, here] = patch_high
        patches[PATCH : 2 * PATCH, here] = patch_low
        patches[2 * PATCH :, here] = patch_high

    slot = lax.broadcasted_iota(jnp.int32, (8, LANES), 0)

    @pl.loop(0, STAMP_COUNT // 4)
    def _(group):
        science = jnp.zeros((STAMP_SIZE, LANES), jnp.float32)
        noise = jnp.ones((STAMP_SIZE, LANES), jnp.float32)
        x_row = jnp.zeros((1, LANES), jnp.float32)
        y_row = jnp.zeros((1, LANES), jnp.float32)
        for member in range(4):
            s = 4 * group + member
            top, left = rows_ref[s], cols_ref[s]
            tile = left // LANES
            tile_start = pl.multiple_of(tile * LANES, LANES)
            next_start = pl.multiple_of(jnp.minimum(tile + 1, COLUMNS // LANES - 1) * LANES, LANES)
            rest = left % LANES
            turn = (LANES + STAMP_SIZE * member - rest) % LANES
            inside = (lane >= STAMP_SIZE * member) & (lane < STAMP_SIZE * (member + 1))
            from_low = lane - STAMP_SIZE * member + rest < LANES
            row_start = pl.multiple_of(jnp.minimum((top // 8) * 8, STRIP_ROWS - CUT_ROWS), 8)
            row_rest = top - row_start
            pieces = []
            for n, ref in enumerate((science_ref, variance_ref)):
                low = pltpu.roll(ref[pl.ds(row_start, CUT_ROWS), pl.ds(tile_start, LANES)], turn, 1)
                high = pltpu.roll(ref[pl.ds(row_start, CUT_ROWS), pl.ds(next_start, LANES)], turn, 1)
                cut_buf[member, n, :, :] = jnp.where(from_low, low, high)
                pieces.append(cut_buf[member, n, pl.ds(row_rest, STAMP_SIZE), :])
            science = jnp.where(inside, pieces[0], science)
            noise = jnp.where(inside, pieces[1], noise)
            col = (left + lane - STAMP_SIZE * member).astype(jnp.float32)
            row = (row_base + top + jnp.zeros_like(lane)).astype(jnp.float32)
            x_row = jnp.where(inside, (2.0 * col + 1.0 - COLUMNS) / COLUMNS, x_row)
            y_row = jnp.where(inside, (2.0 * row + 1.0 - IMAGE_ROWS) / IMAGE_ROWS, y_row)
        sci_buf[...] = science
        wt_buf[...] = lax.rsqrt(noise)
        x = jnp.broadcast_to(x_row, (8, LANES))
        y_first = jnp.broadcast_to(y_row, (8, LANES))
        vert[...] = jnp.dot(
            down_ref[...],
            patches[:, pl.ds(pl.multiple_of(group * 4 * LANES, 4 * LANES), 4 * LANES)],
            preferred_element_type=jnp.float32,
        ).astype(jnp.bfloat16)
        for t, tile in enumerate(TILES):
            out = jnp.dot(
                vert[t * 256 : (t + 1) * 256, :], across_refs[t][...], preferred_element_type=jnp.float32
            )
            out = out.reshape(STAMP_SIZE, 8, len(tile) * LANES)
            value = out[:, :, 0:LANES]
            edge = len(tile[0][1])
            for i in range(1, len(tile)):
                value = jnp.where(slot[None] >= edge, out[:, :, i * LANES : (i + 1) * LANES], value)
                edge += len(tile[i][1])
            if t == CONST_SLOT // 8:
                value = jnp.where(slot[None] == CONST_SLOT % 8, 1.0, value)
            bases[t, :, :, :] = value

        @pl.loop(0, STAMP_SIZE // 4)
        def _(quarter):
            for inner in range(4):
                r = quarter * 4 + inner
                science = jnp.broadcast_to(sci_buf[pl.ds(r, 1), :], (8, LANES))
                weight = jnp.broadcast_to(wt_buf[pl.ds(r, 1), :], (8, LANES))
                tiles = [bases[t, r] for t in range(4)]
                tiles[SCIENCE_SLOT // 8] = jnp.where(
                    slot == SCIENCE_SLOT % 8, science, tiles[SCIENCE_SLOT // 8]
                )
                y = y_first + (2.0 / IMAGE_ROWS) * r.astype(jnp.float32)
                tiles = [b * weight for b in tiles]
                terms = (None, x, y, x * x, x * y, y * y)
                start = pl.multiple_of((group * STAMP_SIZE + r) * LANES, LANES)
                for j, term in enumerate(terms):
                    values = tiles if term is None else [b * term for b in tiles]
                    design[j * SLOTS : (j + 1) * SLOTS, pl.ds(start, LANES)] = jnp.concatenate(
                        values, axis=0
                    ).astype(jnp.bfloat16)

    gram_ref[...] = jnp.zeros_like(gram_ref)

    @pl.loop(0, 16)
    def _(chunk):
        part = design[:, pl.ds(pl.multiple_of(chunk * 1024, 1024), 1024)]
        gram_ref[...] += lax.dot_general(
            part, part, (((1,), (1,)), ((), ())), preferred_element_type=jnp.float32
        )


def down_kernel(down_ref, window_ref, out_ref):
    for block in range(STRIP_ROWS // STAMP_SIZE):
        rows = slice(block * STAMP_SIZE, block * STAMP_SIZE + PATCH)
        piece = jnp.concatenate([window_ref[0, rows, :], window_ref[1, rows, :]], axis=1)
        high = piece.astype(jnp.bfloat16)
        low = (piece - high.astype(jnp.float32)).astype(jnp.bfloat16)
        stacked = jnp.concatenate([high, low, high], axis=0)
        out = jnp.dot(down_ref[...], stacked, preferred_element_type=jnp.float32)
        out_ref[:, block * STAMP_SIZE : (block + 1) * STAMP_SIZE, :] = out.astype(jnp.bfloat16).reshape(
            11, STAMP_SIZE, 2 * LANES
        )


def lane_spread(value, index):
    return jnp.broadcast_to(value[:, index : index + 1], (8, LANES))


def solve(gram_ref):
    row_id = lax.broadcasted_iota(jnp.int32, (8, LANES), 0)
    lane_id = lax.broadcasted_iota(jnp.int32, (8, LANES), 1)
    slots = sorted(s for s, _, _ in slot_of())
    pivots = sorted(slots + [CONST_SLOT])
    active = {32 * j + s for j in range(SPATIAL_TERMS) for s in slots}
    active |= {32 * j + CONST_SLOT for j in range(3)}

    def any_of(ids, chosen):
        mask = jnp.zeros(ids.shape, jnp.bool_)
        for c in chosen:
            mask = mask | (ids == c)
        return mask

    lanes_left = any_of(lane_id, sorted(u for u in active if u < LANES) + [SCIENCE_SLOT])
    lanes_right = any_of(lane_id, [u - LANES for u in sorted(active) if u >= LANES])
    left, right = [], []
    total = jnp.zeros((8, LANES), jnp.float32)
    pad = jnp.zeros((8, 2 * LANES - PADDED), jnp.float32)
    diagonals = []
    for i in range(24):
        rows = any_of(row_id, [u - 8 * i for u in sorted(active) if u // 8 == i])
        a = jnp.where(rows & lanes_left, gram_ref[8 * i : 8 * i + 8, 0:LANES], 0.0)
        b = jnp.concatenate([gram_ref[8 * i : 8 * i + 8, LANES:PADDED], pad], axis=1)
        b = jnp.where(rows & lanes_right, b, 0.0)
        diagonal = lane_id == (row_id + 8 * i) % LANES
        total = total + jnp.where(diagonal & rows, a if i < 16 else b, 0.0)
        left.append(a)
        right.append(b)
        diagonals.append((diagonal, rows))
    ridge = jnp.sum(total, axis=(0, 1), keepdims=True) * (RIDGE / UNKNOWNS)
    for i, (diagonal, rows) in enumerate(diagonals):
        added = jnp.where(diagonal, jnp.where(rows, ridge, 1.0), 0.0)
        if i < 16:
            left[i] = left[i] + jnp.where(lane_id == SCIENCE_SLOT, 0.0, added)
        else:
            right[i] = right[i] + added

    def eliminate(left, right, high):
        left, right = list(left), list(right)
        columns = jnp.concatenate((right if high else left)[4:], axis=0)
        own = [left[:4], right[:4]] if high else [left[:4]]
        lead = len(own) - 1
        for p, q in zip(pivots[0::2], pivots[1::2]):
            rows_p = [jnp.broadcast_to(side[p // 8][p % 8 : p % 8 + 1, :], (8, LANES)) for side in own]
            rows_q = [jnp.broadcast_to(side[q // 8][q % 8 : q % 8 + 1, :], (8, LANES)) for side in own]
            pp, pq = lane_spread(rows_p[lead], p), lane_spread(rows_p[lead], q)
            qp, qq = lane_spread(rows_q[lead], p), lane_spread(rows_q[lead], q)
            scale = 1.0 / (pp * qq - pq * qp)
            pp, pq, qp, qq = pp * scale, pq * scale, qp * scale, qq * scale
            new_p = [qq * first - pq * second for first, second in zip(rows_p, rows_q)]
            new_q = [pp * second - qp * first for first, second in zip(rows_p, rows_q)]
            for i in range(4):
                factor_p = lane_spread(own[lead][i], p)
                factor_q = lane_spread(own[lead][i], q)
                for n, side in enumerate(own):
                    value = side[i] - factor_p * new_p[n] - factor_q * new_q[n]
                    if i == p // 8:
                        value = jnp.where(row_id == p % 8, new_p[n], value)
                    if i == q // 8:
                        value = jnp.where(row_id == q % 8, new_q[n], value)
                    side[i] = value
        rows = jnp.concatenate([jnp.concatenate(side, axis=0) for side in own], axis=1)
        rows = jnp.concatenate([rows, jnp.zeros((LANES - SLOTS, rows.shape[1]), jnp.float32)], axis=0)
        change = jnp.dot(
            columns, rows, precision=lax.Precision.HIGHEST, preferred_element_type=jnp.float32
        )
        for i in range(20):
            part = change[8 * i : 8 * i + 8]
            left[4 + i] = left[4 + i] - part[:, 0:LANES]
            if high:
                right[4 + i] = right[4 + i] - part[:, LANES:]
        left = left[4:] + own[0]
        if high:
            right = [pltpu.roll(v, LANES - SLOTS, 1) for v in right[4:] + own[1]]
        else:
            left = [pltpu.roll(v, LANES - SLOTS, 1) for v in left]
        return tuple(left), tuple(right)

    left, right = left[16:] + left[:16], right[16:] + right[:16]
    left, right = lax.fori_loop(0, 2, lambda _, c: eliminate(c[0], c[1], True), (tuple(left), tuple(right)))
    left = lax.fori_loop(0, 4, lambda _, c: eliminate(c, (), False)[0], left)
    left = left[8:] + left[:8]
    return [lane_spread(v, SCIENCE_SLOT) for v in left]


def model_kernel(row_ref, gram_ref, vert_hbm, science_hbm, *refs):
    across_refs = refs[0:3]
    out_ref = refs[3]
    vert_ref, science_ref, a_buf, b_buf, c_buf, basis_even, basis_odd, copied = refs[4:12]
    copies = (
        pltpu.make_async_copy(vert_hbm, vert_ref, copied.at[0]),
        pltpu.make_async_copy(science_hbm, science_ref, copied.at[1]),
    )
    for copy in copies:
        copy.start()
    solution_tiles = solve(gram_ref)
    lane_id = lax.broadcasted_iota(jnp.int32, (8, LANES), 1)
    row_id = lax.broadcasted_iota(jnp.int32, (8, LANES), 0)
    slots = slot_of()
    group_first = (G0, G1, G2)
    blocks = COLUMNS // LANES
    quarters = STRIP_ROWS // 8
    base = row_ref[0]
    for i in range(blocks):
        x = (2.0 * (lane_id + i * LANES).astype(jnp.float32) + 1.0 - COLUMNS) / COLUMNS
        for t in range(4):
            c = [solution_tiles[4 * j + t] for j in range(SPATIAL_TERMS)]
            a_buf[i, 8 * t : 8 * t + 8, :] = c[0] + x * (c[1] + x * c[3])
            b_buf[i, 8 * t : 8 * t + 8, :] = c[2] + x * c[4]
    def row_position(q):
        return (2.0 * (row_id + 8 * q + base).astype(jnp.float32) + 1.0 - IMAGE_ROWS) / IMAGE_ROWS

    for q in range(quarters):
        y = row_position(q)
        for s, _, _ in slots:
            curve = jnp.broadcast_to(solution_tiles[20 + s // 8][s % 8 : s % 8 + 1, :], (8, LANES))
            c_buf[s, 8 * q : 8 * q + 8, :] = y * curve
    for copy in copies:
        copy.wait()

    def filter_block(pair, f, basis):
        g = 0 if f < 5 else (1 if f < 8 else 2)
        members = [(s, m) for s, ff, m in slots if ff == f]
        start = pl.multiple_of(pair * 2 * LANES, 2 * LANES)
        first = vert_ref[f, :, pl.ds(start, 2 * LANES)]
        second = vert_ref[f, :, pl.ds(pl.multiple_of(start + LANES, LANES), 2 * LANES)]
        out = jnp.dot(
            jnp.concatenate([first, second], axis=0),
            across_refs[g][:, 0 : len(members) * LANES],
            preferred_element_type=jnp.float32,
        )
        for s, m in members:
            k = m - group_first[g]
            basis[s, :, :] = out[:, k * LANES : (k + 1) * LANES]

    def combine(block, half, basis, origin):
        position = [row_position(q) for q in range(quarters)]
        flat = jnp.broadcast_to(a_buf[block, CONST_SLOT : CONST_SLOT + 1, :], (8, LANES))
        slope = jnp.broadcast_to(b_buf[block, CONST_SLOT : CONST_SLOT + 1, :], (8, LANES))
        total = [flat + y * slope for y in position]
        for s, _, _ in slots:
            flat = jnp.broadcast_to(a_buf[block, s : s + 1, :], (8, LANES))
            slope = jnp.broadcast_to(b_buf[block, s : s + 1, :], (8, LANES))
            for q in range(quarters):
                curve = c_buf[origin + s, 8 * q : 8 * q + 8, :]
                field = flat + position[q] * (slope + curve)
                at = STRIP_ROWS * half + 8 * q
                total[q] = total[q] + basis[s, at : at + 8, :] * field
            yield
        columns = pl.ds(pl.multiple_of(block * LANES, LANES), LANES)
        for q in range(quarters):
            rows = slice(8 * q, 8 * q + 8)
            out_ref[rows, columns] = science_ref[rows, columns] - total[q]

    for f in range(11):
        filter_block(0, f, basis_even)

    @pl.loop(0, blocks // 4)
    def _(step):
        for n, (here, there) in enumerate(((basis_even, basis_odd), (basis_odd, basis_even))):
            pair = 2 * step + n
            following = jnp.minimum(pair + 1, blocks // 2 - 1)
            steps = itertools.chain(
                *(combine(2 * pair + half, half, here, row_ref[1 + 2 * n + half]) for half in range(2))
            )
            for f in range(11):
                filter_block(following, f, there)
                for _ in range(5):
                    next(steps, None)
            for _ in steps:
                pass


def exp_steps():
    def place(z, x, y):
        return (z % 2) * 16 + (x % 4) * 4 + y % 4

    def shift(dz, dx, dy):
        return [(place(z, x, y), place(z + dz, x + dx, y + dy)) for z in range(2) for x in range(4) for y in range(4)]

    return shift


def gather_template(piece_a, piece_b):
    shift = exp_steps()

    def move(value, *step):
        return lax.ppermute(value, "exp", shift(*step))

    along_x = ((0, 1, 0), (0, -1, 0), (0, 2, 0))
    along_y = ((0, 0, 1), (0, 0, -1), (0, 0, 2))
    piece = jnp.concatenate([piece_a, piece_b], axis=0)
    other = move(piece, 1, 0, 0)
    both = jnp.stack([piece, other])
    part_a, part_b = both[:, :PIECE_A], both[:, PIECE_A:]
    part_a = jnp.stack([part_a] + [move(part_a, *s) for s in along_y])
    part_b = jnp.stack([part_b] + [move(part_b, *s) for s in along_x])
    parts_a = [part_a] + [move(part_a, *s) for s in along_x]
    parts_b = [part_b] + [move(part_b, *s) for s in along_y]
    return parts_a, parts_b


def reduce_strips(value):
    value = value + lax.ppermute(value, "strip", [(0, 1), (1, 0), (2, 3), (3, 2)])
    return value + lax.ppermute(value, "strip", [(0, 2), (2, 0), (1, 3), (3, 1)])


VMEM = pltpu.MemorySpace.VMEM
SMEM = pltpu.MemorySpace.SMEM


def vmem():
    return pl.BlockSpec(memory_space=VMEM)


def smem():
    return pl.BlockSpec(memory_space=SMEM)


def shards(science, variance, template, offset_rows, offset_cols, stamp_rows, stamp_cols):
    strip_index = lax.axis_index("strip")
    place = lax.axis_index("exp")
    row_base = (strip_index * STRIP_ROWS).astype(jnp.int32)
    piece_a, piece_b = pl.pallas_call(
        pack_kernel,
        out_shape=(
            jax.ShapeDtypeStruct((PIECE_A, LANES), jnp.float32),
            jax.ShapeDtypeStruct((PIECE_B, LANES), jnp.float32),
        ),
        in_specs=[smem(), vmem()],
        out_specs=(vmem(), vmem()),
        name="pack",
    )(strip_index.astype(jnp.int32)[None], template.T)
    parts_a, parts_b = gather_template(piece_a, piece_b)
    scalars = jnp.stack([place.astype(jnp.int32), offset_rows[0], offset_cols[0], row_base])
    gram, window = pl.pallas_call(
        stamps_kernel,
        out_shape=(
            jax.ShapeDtypeStruct((PADDED, PADDED), jnp.float32),
            jax.ShapeDtypeStruct((TILE_COUNT, WINDOW, LANES), jnp.float32),
        ),
        in_specs=[smem()] * 3 + [vmem()] * 15,
        out_specs=(vmem(), vmem()),
        scratch_shapes=[
            pltpu.VMEM((WIDE + 2 * LANES, LANES), jnp.float32),
            pltpu.VMEM((WIDE + 2 * LANES, LANES), jnp.float32),
            pltpu.VMEM((TILE_COUNT, NEED_ROWS + 8, LANES), jnp.float32),
            pltpu.VMEM((3 * PATCH, STAMP_COUNT * LANES), jnp.bfloat16),
            pltpu.VMEM((1024, 4 * LANES), jnp.bfloat16),
            pltpu.VMEM((4, 2, CUT_ROWS, LANES), jnp.float32),
            pltpu.VMEM((STAMP_SIZE, LANES), jnp.float32),
            pltpu.VMEM((STAMP_SIZE, LANES), jnp.float32),
            pltpu.VMEM((4, STAMP_SIZE, 8, LANES), jnp.float32),
            pltpu.VMEM((PADDED, STAMP_COUNT * STAMP_SIZE * STAMP_SIZE), jnp.bfloat16),
        ],
        name="stamps",
    )(
        scalars,
        stamp_rows[0],
        stamp_cols[0],
        *parts_a,
        *parts_b,
        science[0],
        variance[0],
        jnp.asarray(stamp_down()),
        *[jnp.asarray(stamp_across(tile)) for tile in TILES],
    )
    vertical = pl.pallas_call(
        down_kernel,
        out_shape=jax.ShapeDtypeStruct((11, STRIP_ROWS, TILE_COUNT * LANES), jnp.bfloat16),
        grid=(TILE_COUNT // 2,),
        in_specs=[
            pl.BlockSpec((11 * STAMP_SIZE, 3 * PATCH), lambda i: (0, 0)),
            pl.BlockSpec((2, WINDOW, LANES), lambda i: (i, 0, 0)),
        ],
        out_specs=pl.BlockSpec((11, STRIP_ROWS, 2 * LANES), lambda i: (0, 0, i)),
        cost_estimate=pl.CostEstimate(flops=int(4e9), bytes_accessed=int(8e6), transcendentals=0),
        name="down",
    )(jnp.asarray(full_down()), window)
    total = reduce_strips(gram)
    band = across_band(LANES)
    bands = [
        jnp.asarray(band[:, first : first + degree + 1].reshape(2 * LANES, -1))
        for first, degree in zip((G0, G1, G2), DEGREES)
    ]
    result = pl.pallas_call(
        model_kernel,
        out_shape=jax.ShapeDtypeStruct((STRIP_ROWS, COLUMNS), jnp.float32),
        in_specs=[smem(), vmem()] + [pl.BlockSpec(memory_space=pl.ANY)] * 2 + [vmem()] * 3,
        out_specs=vmem(),
        scratch_shapes=[
            pltpu.VMEM((11, STRIP_ROWS, TILE_COUNT * LANES), jnp.bfloat16),
            pltpu.VMEM((STRIP_ROWS, COLUMNS), jnp.float32),
            pltpu.VMEM((COLUMNS // LANES, SLOTS, LANES), jnp.float32),
            pltpu.VMEM((COLUMNS // LANES, SLOTS, LANES), jnp.float32),
            pltpu.VMEM((SLOTS, STRIP_ROWS, LANES), jnp.float32),
            pltpu.VMEM((SLOTS, 2 * STRIP_ROWS, LANES), jnp.float32),
            pltpu.VMEM((SLOTS, 2 * STRIP_ROWS, LANES), jnp.float32),
            pltpu.SemaphoreType.DMA((2,)),
        ],
        name="model",
    )(jnp.stack([row_base] + [row_base * 0] * 4), total, vertical, science[0], *bands)
    return result[None]


def solution(mesh):
    in_specs = (
        P("exp", "strip", None),
        P("exp", "strip", None),
        P(None, "exp"),
        P("exp"),
        P("exp"),
        P("exp", "strip"),
        P("exp", "strip"),
    )
    out_specs = P("exp", "strip", None)
    return jax.shard_map(shards, mesh=mesh, in_specs=in_specs, out_specs=out_specs, check_vma=False)
```

```python
import itertools

import jax
import jax.numpy as jnp
import ml_dtypes
import numpy as np
from jax import lax
from jax.experimental import pallas as pl
from jax.experimental.pallas import tpu as pltpu
from jax.sharding import PartitionSpec as P

STRIP_ROWS = 128
COLUMNS = 2048
IMAGE_ROWS = 512
STAMP_COUNT = 16
STAMP_SIZE = 32
SPATIAL_TERMS = 6
KERNEL_HALF = 20
UNKNOWNS = 165
RIDGE = 0.001
SIGMAS = (1.0, 2.0, 4.0)
DEGREES = (4, 2, 2)

LANES = 128
SOURCE_COLS = 68
NEED_ROWS = 192
WIDE = 2176
TILE_COUNT = 18
PATCH = 80
WINDOW = 176
CUT_ROWS = 40
PIECE_A = 56
PIECE_B = 48

G0, G1, G2 = 0, 5, 8
TILES = (
    ((G0 + 0, (0, 1, 2, 3, 4)), (G0 + 2, (0, 1, 2))),
    ((G0 + 1, (0, 1, 2, 3)), (G0 + 3, (0, 1)), (G0 + 4, (0,))),
    ((G1 + 0, (5, 6, 7)), (G1 + 1, (5, 6)), (G1 + 2, (5,))),
    ((G2 + 0, (8, 9, 10)), (G2 + 1, (8, 9)), (G2 + 2, (8,))),
)
CONST_SLOT = 15
SCIENCE_SLOT = 22
SLOTS = 32
PADDED = SPATIAL_TERMS * SLOTS
POWERS = ((1, 0), (0, 1), (0, 0), (2, 0), (1, 1), (0, 2))
AT_X, AT_Y, AT_ONE, AT_XX, AT_XY, AT_YY = range(SPATIAL_TERMS)
SCIENCE_LANE = SLOTS * AT_ONE + SCIENCE_SLOT
PACKED_ROWS = 5 * SLOTS


def packed_blocks():
    blocks = {}
    for r, left in enumerate(POWERS[2:]):
        for c, right in enumerate(POWERS[:4]):
            blocks.setdefault((left[0] + right[0], left[1] + right[1]), (r, c))
    blocks[(1, 3)] = (4, 0)
    blocks[(0, 4)] = (4, 1)
    return blocks


def tap_table():
    offsets = np.arange(-KERNEL_HALF, KERNEL_HALF + 1).astype(np.float64)
    entries = []
    for spread, degree in zip(SIGMAS, DEGREES):
        profile = np.exp(-offsets * offsets / (2.0 * spread * spread))
        profile = profile / profile.sum()
        for exponent in range(degree + 1):
            entries.append((offsets / spread) ** exponent * profile)
    table = np.stack(entries)
    table[np.abs(table) < 1.2e-38] = 0.0
    return table.astype(np.float32)


def split_halves(table):
    high = table.astype(ml_dtypes.bfloat16)
    low = (table - high.astype(np.float32)).astype(ml_dtypes.bfloat16)
    return high, low


def down_rows(filters, rows):
    taps = tap_table()
    full = np.zeros((len(filters), rows, PATCH), np.float32)
    for i, f in enumerate(filters):
        if f is not None:
            for r in range(rows):
                full[i, r, r : r + 2 * KERNEL_HALF + 1] = taps[f]
    high, low = split_halves(full)
    return np.concatenate([high, high, low], axis=2)


def stamp_down():
    blocks = []
    for tile in TILES:
        filters = [f for _, down in tile for f in down]
        filters += [None] * (8 - len(filters))
        blocks.append(down_rows(filters, STAMP_SIZE).transpose(1, 0, 2).reshape(-1, 3 * PATCH))
    return np.concatenate(blocks)


def full_down():
    return down_rows(list(range(11)), STAMP_SIZE).reshape(-1, 3 * PATCH)


def across_band(width):
    short = tap_table().astype(ml_dtypes.bfloat16)
    band = np.zeros((2 * LANES, 11, width), ml_dtypes.bfloat16)
    for m in range(11):
        for c in range(width):
            band[c : c + 2 * KERNEL_HALF + 1, m, c] = short[m]
    return band


def stamp_across():
    band = across_band(STAMP_SIZE)[:LANES]
    return np.concatenate([np.tile(band[:, m], (1, 4)) for tile in TILES for m, _ in tile], axis=1)


ACROSS_COUNT = sum(len(tile) for tile in TILES)


def slot_of():
    slots = []
    for t, tile in enumerate(TILES):
        s = 8 * t
        for across, down in tile:
            for f in down:
                slots.append((s, f, across))
                s += 1
    return slots


def pack_kernel(strip_ref, template_ref, piece_ref):
    start = pl.multiple_of(strip_ref[0] * LANES, LANES)
    first = template_ref[:, pl.ds(start, LANES)]
    second = template_ref[:, pl.ds(start + LANES, NEED_ROWS - LANES)]
    half = SOURCE_COLS // 2
    piece_ref[0:PIECE_A, :] = first[:PIECE_A]
    piece_ref[PIECE_A + PIECE_B - 8 :, :] = jnp.zeros((8, LANES), jnp.float32)
    piece_ref[PIECE_A : PIECE_A + half, 0:64] = second[:half]
    piece_ref[PIECE_A : PIECE_A + half, 64:128] = second[half:]
    piece_ref[PIECE_A + half : half + SOURCE_COLS, :] = first[PIECE_A:]


def stamps_kernel(scalars, rows_ref, cols_ref, *refs):
    a_refs = refs[0:4]
    b_refs = refs[4:8]
    science_ref, variance_ref, down_ref, across_ref = refs[8:12]
    gram_ref, window_ref = refs[12:14]
    t_one, t_two, w_buf, patches, vert, cut_buf, sci_buf, wt_buf, bases, design, across_buf = refs[14:]
    place, shift_down, shift_side, row_base = scalars[0], scalars[1], scalars[2], scalars[3]
    my_z, my_x, my_y = place // 16, (place // 4) % 4, place % 4
    half = SOURCE_COLS // 2
    offsets = (0, 3, 1, 2)
    for first in range(4):
        for second in range(4):
            for dz in range(2):
                for is_a in (True, False):
                    along_x, along_y = (first, second) if is_a else (second, first)
                    source = (
                        ((my_z + dz) % 2) * 16
                        + ((my_x + offsets[along_x]) % 4) * 4
                        + (my_y + offsets[along_y]) % 4
                    )
                    base = source * SOURCE_COLS
                    if is_a:
                        t_one[pl.ds(base, PIECE_A), :] = a_refs[first][second, dz]
                    else:
                        rest = b_refs[first][second, dz, 0:half, :]
                        t_two[pl.ds(base, half), :] = rest
                        t_two[pl.ds(base + half, half), :] = pltpu.roll(rest, 64, 1)
                        t_one[pl.ds(base + PIECE_A, SOURCE_COLS - PIECE_A), :] = b_refs[first][
                            second, dz, half : half + SOURCE_COLS - PIECE_A, :
                        ]
    t_one[pl.ds(WIDE, 2 * LANES), :] = jnp.zeros((2 * LANES, LANES), jnp.float32)
    t_two[pl.ds(WIDE, 2 * LANES), :] = jnp.zeros((2 * LANES, LANES), jnp.float32)
    w_buf[:, NEED_ROWS:, :] = jnp.zeros((TILE_COUNT, 8, LANES), jnp.float32)

    @pl.loop(0, TILE_COUNT)
    def _(i):
        w_buf[i, 0:LANES, :] = t_one[pl.ds(shift_side + i * LANES, LANES), :].T
        w_buf[i, LANES:NEED_ROWS, :] = t_two[pl.ds(shift_side + i * LANES, LANES), :].T[
            0 : NEED_ROWS - LANES
        ]
        window_ref[i, :, :] = w_buf[i, pl.ds(shift_down, WINDOW), :]

    lane = lax.broadcasted_iota(jnp.int32, (1, LANES), 1)

    @pl.loop(0, STAMP_COUNT)
    def _(s):
        top, left = rows_ref[s], cols_ref[s]
        tile = left // LANES
        rest = left % LANES
        back = (LANES - rest) % LANES
        low = pltpu.roll(window_ref[tile, pl.ds(top, PATCH), :], back, 1)
        high = pltpu.roll(window_ref[tile + 1, pl.ds(top, PATCH), :], back, 1)
        patch = jnp.where(lane < LANES - rest, low, high)
        patch_high = patch.astype(jnp.bfloat16)
        patch_low = (patch - patch_high.astype(jnp.float32)).astype(jnp.bfloat16)
        here = pl.ds(pl.multiple_of(s * LANES, LANES), LANES)
        patches[0:PATCH, here] = patch_high
        patches[PATCH : 2 * PATCH, here] = patch_low
        patches[2 * PATCH :, here] = patch_high

    slot = lax.broadcasted_iota(jnp.int32, (8, LANES), 0)
    for member in range(4):
        own = ((lane >= STAMP_SIZE * member) & (lane < STAMP_SIZE * (member + 1))).astype(jnp.bfloat16)
        for n in range(ACROSS_COUNT):
            here = slice(n * LANES, (n + 1) * LANES)
            across_buf[member * LANES : (member + 1) * LANES, here] = across_ref[:, here] * own

    @pl.loop(0, STAMP_COUNT // 4)
    def _(group):
        science = jnp.zeros((STAMP_SIZE, LANES), jnp.float32)
        noise = jnp.ones((STAMP_SIZE, LANES), jnp.float32)
        x_row = jnp.zeros((1, LANES), jnp.float32)
        y_row = jnp.zeros((1, LANES), jnp.float32)
        for member in range(4):
            s = 4 * group + member
            top, left = rows_ref[s], cols_ref[s]
            tile = left // LANES
            tile_start = pl.multiple_of(tile * LANES, LANES)
            next_start = pl.multiple_of(jnp.minimum(tile + 1, COLUMNS // LANES - 1) * LANES, LANES)
            rest = left % LANES
            turn = (LANES + STAMP_SIZE * member - rest) % LANES
            inside = (lane >= STAMP_SIZE * member) & (lane < STAMP_SIZE * (member + 1))
            from_low = lane - STAMP_SIZE * member + rest < LANES
            row_start = pl.multiple_of(jnp.minimum((top // 8) * 8, STRIP_ROWS - CUT_ROWS), 8)
            row_rest = top - row_start
            pieces = []
            for n, ref in enumerate((science_ref, variance_ref)):
                low = pltpu.roll(ref[pl.ds(row_start, CUT_ROWS), pl.ds(tile_start, LANES)], turn, 1)
                high = pltpu.roll(ref[pl.ds(row_start, CUT_ROWS), pl.ds(next_start, LANES)], turn, 1)
                cut_buf[member, n, :, :] = jnp.where(from_low, low, high)
                pieces.append(cut_buf[member, n, pl.ds(row_rest, STAMP_SIZE), :])
            science = jnp.where(inside, pieces[0], science)
            noise = jnp.where(inside, pieces[1], noise)
            col = (left + lane - STAMP_SIZE * member).astype(jnp.float32)
            row = (row_base + top + jnp.zeros_like(lane)).astype(jnp.float32)
            x_row = jnp.where(inside, (2.0 * col + 1.0 - COLUMNS) / COLUMNS, x_row)
            y_row = jnp.where(inside, (2.0 * row + 1.0 - IMAGE_ROWS) / IMAGE_ROWS, y_row)
        sci_buf[...] = science
        wt_buf[...] = lax.rsqrt(noise)
        x = jnp.broadcast_to(x_row, (8, LANES))
        y_first = jnp.broadcast_to(y_row, (8, LANES))
        vert[...] = jnp.dot(
            down_ref[...],
            patches[:, pl.ds(pl.multiple_of(group * 4 * LANES, 4 * LANES), 4 * LANES)],
            preferred_element_type=jnp.float32,
        ).astype(jnp.bfloat16)
        column = 0
        for t, tile in enumerate(TILES):
            out = jnp.dot(
                vert[t * 256 : (t + 1) * 256, :],
                across_buf[:, column : column + len(tile) * LANES],
                preferred_element_type=jnp.float32,
            )
            column += len(tile) * LANES
            out = out.reshape(STAMP_SIZE, 8, len(tile) * LANES)
            value = out[:, :, 0:LANES]
            edge = len(tile[0][1])
            for i in range(1, len(tile)):
                value = jnp.where(slot[None] >= edge, out[:, :, i * LANES : (i + 1) * LANES], value)
                edge += len(tile[i][1])
            if t == CONST_SLOT // 8:
                value = jnp.where(slot[None] == CONST_SLOT % 8, 1.0, value)
            bases[t, :, :, :] = value

        @pl.loop(0, STAMP_SIZE // 4)
        def _(quarter):
            for inner in range(4):
                r = quarter * 4 + inner
                science = jnp.broadcast_to(sci_buf[pl.ds(r, 1), :], (8, LANES))
                weight = jnp.broadcast_to(wt_buf[pl.ds(r, 1), :], (8, LANES))
                tiles = [bases[t, r] for t in range(4)]
                tiles[SCIENCE_SLOT // 8] = jnp.where(
                    slot == SCIENCE_SLOT % 8, science, tiles[SCIENCE_SLOT // 8]
                )
                y = y_first + (2.0 / IMAGE_ROWS) * r.astype(jnp.float32)
                tiles = [b * weight for b in tiles]
                terms = (x, y, None, x * x, x * y, y * y)
                start = pl.multiple_of((group * STAMP_SIZE + r) * LANES, LANES)
                for j, term in enumerate(terms):
                    values = tiles if term is None else [b * term for b in tiles]
                    design[j * SLOTS : (j + 1) * SLOTS, pl.ds(start, LANES)] = jnp.concatenate(
                        values, axis=0
                    ).astype(jnp.bfloat16)

    gram_ref[...] = jnp.zeros_like(gram_ref)
    across_pixels = (((1,), (1,)), ((), ()))

    @pl.loop(0, 8)
    def _(chunk):
        here = pl.ds(pl.multiple_of(chunk * 2048, 2048), 2048)
        gram_ref[0:LANES, :] += lax.dot_general(
            design[PADDED - LANES :, here],
            design[0:LANES, here],
            across_pixels,
            preferred_element_type=jnp.float32,
        )
        rest = lax.dot_general(
            design[PADDED - SLOTS :, here],
            design[PADDED - 2 * SLOTS :, here],
            across_pixels,
            preferred_element_type=jnp.float32,
        )
        gram_ref[LANES:, 0 : 2 * SLOTS] += rest


def lane_spread(value, index):
    return jnp.take_along_axis(value, jnp.full((8, LANES), index, jnp.int32), axis=1)


def row_spread(tiles, index):
    return jnp.broadcast_to(tiles[index // 8][index % 8 : index % 8 + 1, :], (8, LANES))


def solve(gram_ref, beside):
    row_id = lax.broadcasted_iota(jnp.int32, (8, LANES), 0)
    lane_id = lax.broadcasted_iota(jnp.int32, (8, LANES), 1)
    slots = sorted(s for s, _, _ in slot_of())
    pivots = sorted(slots + [CONST_SLOT])
    active = {32 * j + s for j in range(SPATIAL_TERMS) for s in slots}
    active |= {32 * j + CONST_SLOT for j in range(3)}

    def any_of(ids, chosen):
        mask = jnp.zeros(ids.shape, jnp.bool_)
        for c in chosen:
            mask = mask | (ids == c)
        return mask

    lanes_left = any_of(lane_id, sorted(u for u in active if u < LANES) + [SCIENCE_LANE])
    lanes_right = any_of(lane_id, [u - LANES for u in sorted(active) if u >= LANES])
    left, right = [], []
    total = jnp.zeros((8, LANES), jnp.float32)
    diagonals = []
    blocks = packed_blocks()
    packed = [gram_ref[8 * i : 8 * i + 8, :] for i in range(PACKED_ROWS // 8)]

    def gathered(i, columns):
        own = POWERS[i // 4]
        out = None
        for place, column in enumerate(columns):
            row, lane = blocks[(own[0] + POWERS[column][0], own[1] + POWERS[column][1])]
            source = packed[4 * row + i % 4]
            if place != lane:
                source = pltpu.roll(source, (SLOTS * (place - lane)) % LANES, 1)
            out = source if out is None else jnp.where(lane_id >= SLOTS * place, source, out)
        return out

    for i in range(24):
        rows = any_of(row_id, [u - 8 * i for u in sorted(active) if u // 8 == i])
        whole = packed[4 * (i // 4 - 2) + i % 4] if i >= 8 else gathered(i, (0, 1, 2, 3))
        a = jnp.where(rows & lanes_left, whole, 0.0)
        b = jnp.where(rows & lanes_right, gathered(i, (4, 5)), 0.0)
        diagonal = lane_id == (row_id + 8 * i) % LANES
        total = total + jnp.where(diagonal & rows, a if i < 16 else b, 0.0)
        left.append(a)
        right.append(b)
        diagonals.append((diagonal, rows))
    ridge = jnp.sum(total, axis=(0, 1), keepdims=True) * (RIDGE / UNKNOWNS)
    for i, (diagonal, rows) in enumerate(diagonals):
        added = jnp.where(diagonal, jnp.where(rows, ridge, 1.0), 0.0)
        if i < 16:
            left[i] = left[i] + jnp.where(lane_id == SCIENCE_LANE, 0.0, added)
        else:
            right[i] = right[i] + added

    def eliminate(left, right, high):
        left, right = list(left), list(right)
        columns = jnp.concatenate((right if high else left)[4:], axis=0)
        own = [left[:4], right[:4]] if high else [left[:4]]
        lead = len(own) - 1
        for p, q in zip(pivots[0::2], pivots[1::2]):
            factor_p = [lane_spread(own[lead][i], p) for i in range(4)]
            factor_q = [lane_spread(own[lead][i], q) for i in range(4)]
            rows_p = [row_spread(side, p) for side in own]
            rows_q = [row_spread(side, q) for side in own]
            pp, pq = row_spread(factor_p, p), row_spread(factor_q, p)
            qp, qq = row_spread(factor_p, q), row_spread(factor_q, q)
            scale = 1.0 / (pp * qq - pq * qp)
            new_p = [(qq * first - pq * second) * scale for first, second in zip(rows_p, rows_q)]
            new_q = [(pp * second - qp * first) * scale for first, second in zip(rows_p, rows_q)]
            for i in range(4):
                for n, side in enumerate(own):
                    value = side[i] - factor_p[i] * new_p[n] - factor_q[i] * new_q[n]
                    if i == p // 8:
                        value = jnp.where(row_id == p % 8, new_p[n], value)
                    if i == q // 8:
                        value = jnp.where(row_id == q % 8, new_q[n], value)
                    side[i] = value
        rows = jnp.concatenate([jnp.concatenate(side, axis=0) for side in own], axis=1)
        rows = jnp.concatenate([rows, jnp.zeros((LANES - SLOTS, rows.shape[1]), jnp.float32)], axis=0)
        change = jnp.dot(
            columns, rows, precision=lax.Precision.HIGHEST, preferred_element_type=jnp.float32
        )
        for i in range(20):
            part = change[8 * i : 8 * i + 8]
            left[4 + i] = left[4 + i] - part[:, 0:LANES]
            if high:
                right[4 + i] = right[4 + i] - part[:, LANES:]
        left = left[4:] + own[0]
        if high:
            right = [pltpu.roll(v, LANES - SLOTS, 1) for v in right[4:] + own[1]]
        else:
            left = [pltpu.roll(v, LANES - SLOTS, 1) for v in left]
        return tuple(left), tuple(right)

    left, right = left[16:] + left[:16], right[16:] + right[:16]

    def both_sides(step, carry):
        beside(step)
        return eliminate(carry[0], carry[1], True)

    def left_side(step, carry):
        beside(2 * step + 2)
        beside(2 * step + 3)
        return eliminate(carry, (), False)[0]

    left, right = lax.fori_loop(0, 2, both_sides, (tuple(left), tuple(right)))
    left = lax.fori_loop(0, 4, left_side, left)
    left = left[8:] + left[:8]
    return [lane_spread(v, SCIENCE_LANE) for v in left]


def model_kernel(row_ref, gram_ref, window_ref, down_ref, science_ref, *refs):
    across_refs = refs[0:3]
    out_ref = refs[3]
    vert_ref, a_buf, b_buf, c_buf, basis_even, basis_odd = refs[4:10]

    def filter_down(step):
        pair = jnp.minimum(step, TILE_COUNT // 2 - 1)
        columns = pl.ds(pl.multiple_of(pair * 2 * LANES, 2 * LANES), 2 * LANES)
        for block in range(STRIP_ROWS // STAMP_SIZE):
            rows = slice(block * STAMP_SIZE, block * STAMP_SIZE + PATCH)
            piece = jnp.concatenate([window_ref[2 * pair, rows, :], window_ref[2 * pair + 1, rows, :]], axis=1)
            high = piece.astype(jnp.bfloat16)
            low = (piece - high.astype(jnp.float32)).astype(jnp.bfloat16)
            stacked = jnp.concatenate([high, low, high], axis=0)
            out = jnp.dot(down_ref[...], stacked, preferred_element_type=jnp.float32)
            vert_ref[:, block * STAMP_SIZE : (block + 1) * STAMP_SIZE, columns] = out.astype(
                jnp.bfloat16
            ).reshape(11, STAMP_SIZE, 2 * LANES)

    solution_tiles = solve(gram_ref, filter_down)
    lane_id = lax.broadcasted_iota(jnp.int32, (8, LANES), 1)
    row_id = lax.broadcasted_iota(jnp.int32, (8, LANES), 0)
    slots = slot_of()
    group_first = (G0, G1, G2)
    blocks = COLUMNS // LANES
    quarters = STRIP_ROWS // 8
    base = row_ref[0]
    for i in range(blocks):
        x = (2.0 * (lane_id + i * LANES).astype(jnp.float32) + 1.0 - COLUMNS) / COLUMNS
        for t in range(4):
            c = [solution_tiles[4 * j + t] for j in range(SPATIAL_TERMS)]
            a_buf[i, 8 * t : 8 * t + 8, :] = c[AT_ONE] + x * (c[AT_X] + x * c[AT_XX])
            b_buf[i, 8 * t : 8 * t + 8, :] = c[AT_Y] + x * c[AT_XY]
    def row_position(q):
        return (2.0 * (row_id + 8 * q + base).astype(jnp.float32) + 1.0 - IMAGE_ROWS) / IMAGE_ROWS

    for q in range(quarters):
        y = row_position(q)
        for s, _, _ in slots:
            curve = jnp.broadcast_to(solution_tiles[4 * AT_YY + s // 8][s % 8 : s % 8 + 1, :], (8, LANES))
            c_buf[s, 8 * q : 8 * q + 8, :] = y * curve

    def filter_block(pair, f, basis):
        g = 0 if f < 5 else (1 if f < 8 else 2)
        members = [(s, m) for s, ff, m in slots if ff == f]
        start = pl.multiple_of(pair * 2 * LANES, 2 * LANES)
        first = vert_ref[f, :, pl.ds(start, 2 * LANES)]
        second = vert_ref[f, :, pl.ds(pl.multiple_of(start + LANES, LANES), 2 * LANES)]
        out = jnp.dot(
            jnp.concatenate([first, second], axis=0),
            across_refs[g][:, 0 : len(members) * LANES],
            preferred_element_type=jnp.float32,
        )
        for s, m in members:
            k = m - group_first[g]
            basis[s, :, :] = out[:, k * LANES : (k + 1) * LANES]

    def combine(block, half, basis, origin):
        position = [row_position(q) for q in range(quarters)]
        flat = jnp.broadcast_to(a_buf[block, CONST_SLOT : CONST_SLOT + 1, :], (8, LANES))
        slope = jnp.broadcast_to(b_buf[block, CONST_SLOT : CONST_SLOT + 1, :], (8, LANES))
        total = [flat + y * slope for y in position]
        for s, _, _ in slots:
            flat = jnp.broadcast_to(a_buf[block, s : s + 1, :], (8, LANES))
            slope = jnp.broadcast_to(b_buf[block, s : s + 1, :], (8, LANES))
            for q in range(quarters):
                curve = c_buf[origin + s, 8 * q : 8 * q + 8, :]
                field = flat + position[q] * (slope + curve)
                at = STRIP_ROWS * half + 8 * q
                total[q] = total[q] + basis[s, at : at + 8, :] * field
            yield
        columns = pl.ds(pl.multiple_of(block * LANES, LANES), LANES)
        for q in range(quarters):
            rows = slice(8 * q, 8 * q + 8)
            out_ref[rows, columns] = science_ref[rows, columns] - total[q]

    for f in range(11):
        filter_block(0, f, basis_even)

    @pl.loop(0, blocks // 4)
    def _(step):
        for n, (here, there) in enumerate(((basis_even, basis_odd), (basis_odd, basis_even))):
            pair = 2 * step + n
            following = jnp.minimum(pair + 1, blocks // 2 - 1)
            steps = itertools.chain(
                *(combine(2 * pair + half, half, here, row_ref[1 + 2 * n + half]) for half in range(2))
            )
            for f in range(11):
                filter_block(following, f, there)
                for _ in range(5):
                    next(steps, None)
            for _ in steps:
                pass


def exp_steps():
    def place(z, x, y):
        return (z % 2) * 16 + (x % 4) * 4 + y % 4

    def shift(dz, dx, dy):
        return [(place(z, x, y), place(z + dz, x + dx, y + dy)) for z in range(2) for x in range(4) for y in range(4)]

    return shift


def gather_template(piece):
    shift = exp_steps()

    def move(value, *step):
        return lax.ppermute(value, "exp", shift(*step))

    along_x = ((0, 1, 0), (0, -1, 0), (0, 2, 0))
    along_y = ((0, 0, 1), (0, 0, -1), (0, 0, 2))
    other = move(piece, 1, 0, 0)
    both = lax.optimization_barrier(jnp.stack([piece, other]))
    part_a, part_b = both[:, :PIECE_A], both[:, PIECE_A:]
    part_a = jnp.stack([part_a] + [move(part_a, *s) for s in along_y])
    part_b = jnp.stack([part_b] + [move(part_b, *s) for s in along_x])
    parts_a = [part_a] + [move(part_a, *s) for s in along_x]
    parts_b = [part_b] + [move(part_b, *s) for s in along_y]
    return parts_a, parts_b


def reduce_strips(value):
    value = value + lax.ppermute(value, "strip", [(0, 1), (1, 0), (2, 3), (3, 2)])
    return value + lax.ppermute(value, "strip", [(0, 2), (2, 0), (1, 3), (3, 1)])


VMEM = pltpu.MemorySpace.VMEM
SMEM = pltpu.MemorySpace.SMEM


def kept(value):
    return pltpu.with_memory_space_constraint(value, VMEM)


def vmem():
    return pl.BlockSpec(memory_space=VMEM)


def smem():
    return pl.BlockSpec(memory_space=SMEM)


def shards(science, variance, template, offset_rows, offset_cols, stamp_rows, stamp_cols):
    strip_index = lax.axis_index("strip")
    place = lax.axis_index("exp")
    row_base = (strip_index * STRIP_ROWS).astype(jnp.int32)
    picture = kept(science[0])
    piece = pl.pallas_call(
        pack_kernel,
        out_shape=pltpu.VMEM((PIECE_A + PIECE_B, LANES), jnp.float32),
        in_specs=[smem(), vmem()],
        out_specs=vmem(),
        name="pack",
    )(strip_index.astype(jnp.int32)[None], template.T)
    parts_a, parts_b = gather_template(piece)
    scalars = jnp.stack([place.astype(jnp.int32), offset_rows[0], offset_cols[0], row_base])
    gram, window = pl.pallas_call(
        stamps_kernel,
        out_shape=(
            pltpu.VMEM((PACKED_ROWS, LANES), jnp.float32),
            pltpu.VMEM((TILE_COUNT, WINDOW, LANES), jnp.float32),
        ),
        in_specs=[smem()] * 3 + [vmem()] * 12,
        out_specs=(vmem(), vmem()),
        scratch_shapes=[
            pltpu.VMEM((WIDE + 2 * LANES, LANES), jnp.float32),
            pltpu.VMEM((WIDE + 2 * LANES, LANES), jnp.float32),
            pltpu.VMEM((TILE_COUNT, NEED_ROWS + 8, LANES), jnp.float32),
            pltpu.VMEM((3 * PATCH, STAMP_COUNT * LANES), jnp.bfloat16),
            pltpu.VMEM((1024, 4 * LANES), jnp.bfloat16),
            pltpu.VMEM((4, 2, CUT_ROWS, LANES), jnp.float32),
            pltpu.VMEM((STAMP_SIZE, LANES), jnp.float32),
            pltpu.VMEM((STAMP_SIZE, LANES), jnp.float32),
            pltpu.VMEM((4, STAMP_SIZE, 8, LANES), jnp.float32),
            pltpu.VMEM((PADDED, STAMP_COUNT * STAMP_SIZE * STAMP_SIZE), jnp.bfloat16),
            pltpu.VMEM((4 * LANES, ACROSS_COUNT * LANES), jnp.bfloat16),
        ],
        compiler_params=pltpu.CompilerParams(vmem_limit_bytes=28 << 20),
        name="stamps",
    )(
        scalars,
        stamp_rows[0],
        stamp_cols[0],
        *[kept(part) for part in parts_a + parts_b],
        picture,
        kept(variance[0]),
        kept(jnp.asarray(stamp_down())),
        kept(jnp.asarray(stamp_across())),
    )
    total = reduce_strips(gram)
    band = across_band(LANES)
    bands = [
        kept(jnp.asarray(band[:, first : first + degree + 1].reshape(2 * LANES, -1)))
        for first, degree in zip((G0, G1, G2), DEGREES)
    ]
    result = pl.pallas_call(
        model_kernel,
        out_shape=jax.ShapeDtypeStruct((STRIP_ROWS, COLUMNS), jnp.float32),
        in_specs=[smem()] + [vmem()] * 7,
        out_specs=vmem(),
        scratch_shapes=[
            pltpu.VMEM((11, STRIP_ROWS, TILE_COUNT * LANES), jnp.bfloat16),
            pltpu.VMEM((COLUMNS // LANES, SLOTS, LANES), jnp.float32),
            pltpu.VMEM((COLUMNS // LANES, SLOTS, LANES), jnp.float32),
            pltpu.VMEM((SLOTS, STRIP_ROWS, LANES), jnp.float32),
            pltpu.VMEM((SLOTS, 2 * STRIP_ROWS, LANES), jnp.float32),
            pltpu.VMEM((SLOTS, 2 * STRIP_ROWS, LANES), jnp.float32),
        ],
        compiler_params=pltpu.CompilerParams(vmem_limit_bytes=32 << 20),
        name="model",
    )(jnp.stack([row_base] + [row_base * 0] * 4), kept(total), window, kept(jnp.asarray(full_down())), picture, *bands)
    return result[None]


def solution(mesh):
    in_specs = (
        P("exp", "strip", None),
        P("exp", "strip", None),
        P(None, "exp"),
        P("exp"),
        P("exp"),
        P("exp", "strip"),
        P("exp", "strip"),
    )
    out_specs = P("exp", "strip", None)
    return jax.shard_map(shards, mesh=mesh, in_specs=in_specs, out_specs=out_specs, check_vma=False)
```

```python
import itertools

import jax
import jax.numpy as jnp
import ml_dtypes
import numpy as np
from jax import lax
from jax.experimental import pallas as pl
from jax.experimental.pallas import tpu as pltpu
from jax.sharding import PartitionSpec as P

STRIP_ROWS = 128
COLUMNS = 2048
IMAGE_ROWS = 512
STAMP_COUNT = 16
STAMP_SIZE = 32
SPATIAL_TERMS = 6
KERNEL_HALF = 20
UNKNOWNS = 165
RIDGE = 0.001
SIGMAS = (1.0, 2.0, 4.0)
DEGREES = (4, 2, 2)

LANES = 128
SOURCE_COLS = 68
NEED_ROWS = 192
WIDE = 2176
TILE_COUNT = 18
PATCH = 80
WINDOW = 176
CUT_ROWS = 40
PIECE_A = 56
PIECE_B = 48

G0, G1, G2 = 0, 5, 8
TILES = (
    ((G0 + 0, (0, 1, 2, 3, 4)), (G0 + 2, (0, 1, 2))),
    ((G0 + 1, (0, 1, 2, 3)), (G0 + 3, (0, 1)), (G0 + 4, (0,))),
    ((G1 + 0, (5, 6, 7)), (G1 + 1, (5, 6)), (G1 + 2, (5,))),
    ((G2 + 0, (8, 9, 10)), (G2 + 1, (8, 9)), (G2 + 2, (8,))),
)
CONST_SLOT = 15
SCIENCE_SLOT = 22
SLOTS = 32
PADDED = SPATIAL_TERMS * SLOTS
POWERS = ((1, 0), (0, 1), (0, 0), (2, 0), (1, 1), (0, 2))
AT_X, AT_Y, AT_ONE, AT_XX, AT_XY, AT_YY = range(SPATIAL_TERMS)
SCIENCE_LANE = SLOTS * AT_ONE + SCIENCE_SLOT
PACKED_ROWS = 5 * SLOTS


def packed_blocks():
    blocks = {}
    for r, left in enumerate(POWERS[2:]):
        for c, right in enumerate(POWERS[:4]):
            blocks.setdefault((left[0] + right[0], left[1] + right[1]), (r, c))
    blocks[(1, 3)] = (4, 0)
    blocks[(0, 4)] = (4, 1)
    return blocks


def tap_table():
    offsets = np.arange(-KERNEL_HALF, KERNEL_HALF + 1).astype(np.float64)
    entries = []
    for spread, degree in zip(SIGMAS, DEGREES):
        profile = np.exp(-offsets * offsets / (2.0 * spread * spread))
        profile = profile / profile.sum()
        for exponent in range(degree + 1):
            entries.append((offsets / spread) ** exponent * profile)
    table = np.stack(entries)
    table[np.abs(table) < 1.2e-38] = 0.0
    return table.astype(np.float32)


def split_halves(table):
    high = table.astype(ml_dtypes.bfloat16)
    low = (table - high.astype(np.float32)).astype(ml_dtypes.bfloat16)
    return high, low


def down_rows(filters, rows):
    taps = tap_table()
    full = np.zeros((len(filters), rows, PATCH), np.float32)
    for i, f in enumerate(filters):
        if f is not None:
            for r in range(rows):
                full[i, r, r : r + 2 * KERNEL_HALF + 1] = taps[f]
    high, low = split_halves(full)
    return np.concatenate([high, high, low], axis=2)


def stamp_down():
    blocks = []
    for tile in TILES:
        filters = [f for _, down in tile for f in down]
        filters += [None] * (8 - len(filters))
        blocks.append(down_rows(filters, STAMP_SIZE).transpose(1, 0, 2).reshape(-1, 3 * PATCH))
    return np.concatenate(blocks)


def full_down():
    return down_rows(list(range(11)), STAMP_SIZE).reshape(-1, 3 * PATCH)


def across_band(width):
    short = tap_table().astype(ml_dtypes.bfloat16)
    band = np.zeros((2 * LANES, 11, width), ml_dtypes.bfloat16)
    for m in range(11):
        for c in range(width):
            band[c : c + 2 * KERNEL_HALF + 1, m, c] = short[m]
    return band


def stamp_across():
    band = across_band(STAMP_SIZE)[:LANES]
    return np.concatenate([np.tile(band[:, m], (1, 4)) for tile in TILES for m, _ in tile], axis=1)


ACROSS_COUNT = sum(len(tile) for tile in TILES)


def slot_of():
    slots = []
    for t, tile in enumerate(TILES):
        s = 8 * t
        for across, down in tile:
            for f in down:
                slots.append((s, f, across))
                s += 1
    return slots


def pack_kernel(strip_ref, template_ref, piece_ref):
    start = pl.multiple_of(strip_ref[0] * LANES, LANES)
    first = template_ref[:, pl.ds(start, LANES)]
    second = template_ref[:, pl.ds(start + LANES, NEED_ROWS - LANES)]
    half = SOURCE_COLS // 2
    piece_ref[0:PIECE_A, :] = first[:PIECE_A]
    piece_ref[PIECE_A + PIECE_B - 8 :, :] = jnp.zeros((8, LANES), jnp.float32)
    piece_ref[PIECE_A : PIECE_A + half, 0:64] = second[:half]
    piece_ref[PIECE_A : PIECE_A + half, 64:128] = second[half:]
    piece_ref[PIECE_A + half : half + SOURCE_COLS, :] = first[PIECE_A:]


def stamps_kernel(scalars, rows_ref, cols_ref, *refs):
    a_refs = refs[0:4]
    b_refs = refs[4:8]
    science_ref, variance_ref, down_ref, across_ref = refs[8:12]
    gram_ref, window_ref = refs[12:14]
    t_one, t_two, w_buf, patches, vert, cut_buf, sci_buf, wt_buf, bases, design, across_buf = refs[14:25]
    variance_buf, copied = refs[25:]
    copy = pltpu.make_async_copy(variance_ref, variance_buf, copied)
    copy.start()
    place, shift_down, shift_side, row_base = scalars[0], scalars[1], scalars[2], scalars[3]
    my_z, my_x, my_y = place // 16, (place // 4) % 4, place % 4
    half = SOURCE_COLS // 2
    def direct(own):
        return (own, (own + 3) % 4, (own + 1) % 4, (own + 2) % 4)

    def doubled(own):
        near = own + 1 - 2 * (own % 2)
        return (own, near, 3 - own, 3 - near)

    for first in range(4):
        for second in range(4):
            for dz in range(2):
                for is_a in (True, False):
                    along_x = direct(my_x)[first] if is_a else doubled(my_x)[second]
                    along_y = doubled(my_y)[second] if is_a else direct(my_y)[first]
                    source = ((my_z + dz) % 2) * 16 + along_x * 4 + along_y
                    base = source * SOURCE_COLS
                    if is_a:
                        t_one[pl.ds(base, PIECE_A), :] = a_refs[first][second, dz]
                    else:
                        rest = b_refs[first][second, dz, 0:half, :]
                        t_two[pl.ds(base, half), :] = rest
                        t_two[pl.ds(base + half, half), :] = pltpu.roll(rest, 64, 1)
                        t_one[pl.ds(base + PIECE_A, SOURCE_COLS - PIECE_A), :] = b_refs[first][
                            second, dz, half : half + SOURCE_COLS - PIECE_A, :
                        ]
    t_one[pl.ds(WIDE, 2 * LANES), :] = jnp.zeros((2 * LANES, LANES), jnp.float32)
    t_two[pl.ds(WIDE, 2 * LANES), :] = jnp.zeros((2 * LANES, LANES), jnp.float32)
    w_buf[:, NEED_ROWS:, :] = jnp.zeros((TILE_COUNT, 8, LANES), jnp.float32)

    @pl.loop(0, TILE_COUNT)
    def _(i):
        w_buf[i, 0:LANES, :] = t_one[pl.ds(shift_side + i * LANES, LANES), :].T
        w_buf[i, LANES:NEED_ROWS, :] = t_two[pl.ds(shift_side + i * LANES, LANES), :].T[
            0 : NEED_ROWS - LANES
        ]
        window_ref[i, :, :] = w_buf[i, pl.ds(shift_down, WINDOW), :]

    lane = lax.broadcasted_iota(jnp.int32, (1, LANES), 1)

    @pl.loop(0, STAMP_COUNT)
    def _(s):
        top, left = rows_ref[s], cols_ref[s]
        tile = left // LANES
        rest = left % LANES
        back = (LANES - rest) % LANES
        low = pltpu.roll(window_ref[tile, pl.ds(top, PATCH), :], back, 1)
        high = pltpu.roll(window_ref[tile + 1, pl.ds(top, PATCH), :], back, 1)
        patch = jnp.where(lane < LANES - rest, low, high)
        patch_high = patch.astype(jnp.bfloat16)
        patch_low = (patch - patch_high.astype(jnp.float32)).astype(jnp.bfloat16)
        here = pl.ds(pl.multiple_of(s * LANES, LANES), LANES)
        patches[0:PATCH, here] = patch_high
        patches[PATCH : 2 * PATCH, here] = patch_low
        patches[2 * PATCH :, here] = patch_high

    copy.wait()
    slot = lax.broadcasted_iota(jnp.int32, (8, LANES), 0)
    for member in range(4):
        own = ((lane >= STAMP_SIZE * member) & (lane < STAMP_SIZE * (member + 1))).astype(jnp.bfloat16)
        for n in range(ACROSS_COUNT):
            here = slice(n * LANES, (n + 1) * LANES)
            across_buf[member * LANES : (member + 1) * LANES, here] = across_ref[:, here] * own

    @pl.loop(0, STAMP_COUNT // 4)
    def _(group):
        science = jnp.zeros((STAMP_SIZE, LANES), jnp.float32)
        noise = jnp.ones((STAMP_SIZE, LANES), jnp.float32)
        x_row = jnp.zeros((1, LANES), jnp.float32)
        y_row = jnp.zeros((1, LANES), jnp.float32)
        for member in range(4):
            s = 4 * group + member
            top, left = rows_ref[s], cols_ref[s]
            tile = left // LANES
            tile_start = pl.multiple_of(tile * LANES, LANES)
            next_start = pl.multiple_of(jnp.minimum(tile + 1, COLUMNS // LANES - 1) * LANES, LANES)
            rest = left % LANES
            turn = (LANES + STAMP_SIZE * member - rest) % LANES
            inside = (lane >= STAMP_SIZE * member) & (lane < STAMP_SIZE * (member + 1))
            from_low = lane - STAMP_SIZE * member + rest < LANES
            row_start = pl.multiple_of(jnp.minimum((top // 8) * 8, STRIP_ROWS - CUT_ROWS), 8)
            row_rest = top - row_start
            pieces = []
            for n, ref in enumerate((science_ref, variance_buf)):
                low = pltpu.roll(ref[pl.ds(row_start, CUT_ROWS), pl.ds(tile_start, LANES)], turn, 1)
                high = pltpu.roll(ref[pl.ds(row_start, CUT_ROWS), pl.ds(next_start, LANES)], turn, 1)
                cut_buf[member, n, :, :] = jnp.where(from_low, low, high)
                pieces.append(cut_buf[member, n, pl.ds(row_rest, STAMP_SIZE), :])
            science = jnp.where(inside, pieces[0], science)
            noise = jnp.where(inside, pieces[1], noise)
            col = (left + lane - STAMP_SIZE * member).astype(jnp.float32)
            row = (row_base + top + jnp.zeros_like(lane)).astype(jnp.float32)
            x_row = jnp.where(inside, (2.0 * col + 1.0 - COLUMNS) / COLUMNS, x_row)
            y_row = jnp.where(inside, (2.0 * row + 1.0 - IMAGE_ROWS) / IMAGE_ROWS, y_row)
        sci_buf[...] = science
        wt_buf[...] = lax.rsqrt(noise)
        x = jnp.broadcast_to(x_row, (8, LANES))
        y_first = jnp.broadcast_to(y_row, (8, LANES))
        vert[...] = jnp.dot(
            down_ref[...],
            patches[:, pl.ds(pl.multiple_of(group * 4 * LANES, 4 * LANES), 4 * LANES)],
            preferred_element_type=jnp.float32,
        ).astype(jnp.bfloat16)
        column = 0
        for t, tile in enumerate(TILES):
            out = jnp.dot(
                vert[t * 256 : (t + 1) * 256, :],
                across_buf[:, column : column + len(tile) * LANES],
                preferred_element_type=jnp.float32,
            )
            column += len(tile) * LANES
            out = out.reshape(STAMP_SIZE, 8, len(tile) * LANES)
            value = out[:, :, 0:LANES]
            edge = len(tile[0][1])
            for i in range(1, len(tile)):
                value = jnp.where(slot[None] >= edge, out[:, :, i * LANES : (i + 1) * LANES], value)
                edge += len(tile[i][1])
            if t == CONST_SLOT // 8:
                value = jnp.where(slot[None] == CONST_SLOT % 8, 1.0, value)
            bases[t, :, :, :] = value

        @pl.loop(0, STAMP_SIZE // 4)
        def _(quarter):
            for inner in range(4):
                r = quarter * 4 + inner
                science = jnp.broadcast_to(sci_buf[pl.ds(r, 1), :], (8, LANES))
                weight = jnp.broadcast_to(wt_buf[pl.ds(r, 1), :], (8, LANES))
                tiles = [bases[t, r] for t in range(4)]
                tiles[SCIENCE_SLOT // 8] = jnp.where(
                    slot == SCIENCE_SLOT % 8, science, tiles[SCIENCE_SLOT // 8]
                )
                y = y_first + (2.0 / IMAGE_ROWS) * r.astype(jnp.float32)
                tiles = [b * weight for b in tiles]
                terms = (x, y, None, x * x, x * y, y * y)
                start = pl.multiple_of((group * STAMP_SIZE + r) * LANES, LANES)
                for j, term in enumerate(terms):
                    values = tiles if term is None else [b * term for b in tiles]
                    design[j * SLOTS : (j + 1) * SLOTS, pl.ds(start, LANES)] = jnp.concatenate(
                        values, axis=0
                    ).astype(jnp.bfloat16)

    gram_ref[...] = jnp.zeros_like(gram_ref)
    across_pixels = (((1,), (1,)), ((), ()))

    @pl.loop(0, 8)
    def _(chunk):
        here = pl.ds(pl.multiple_of(chunk * 2048, 2048), 2048)
        gram_ref[0:LANES, :] += lax.dot_general(
            design[PADDED - LANES :, here],
            design[0:LANES, here],
            across_pixels,
            preferred_element_type=jnp.float32,
        )
        rest = lax.dot_general(
            design[PADDED - SLOTS :, here],
            design[PADDED - 2 * SLOTS :, here],
            across_pixels,
            preferred_element_type=jnp.float32,
        )
        gram_ref[LANES:, 0 : 2 * SLOTS] += rest


def lane_spread(value, index):
    return jnp.take_along_axis(value, jnp.full((8, LANES), index, jnp.int32), axis=1)


def spread_column(tiles, index):
    return [lane_spread(v, index) for v in tiles]


def row_spread(tiles, index):
    return jnp.broadcast_to(tiles[index // 8][index % 8 : index % 8 + 1, :], (8, LANES))


def solve(gram_ref, beside, first_block):
    row_id = lax.broadcasted_iota(jnp.int32, (8, LANES), 0)
    lane_id = lax.broadcasted_iota(jnp.int32, (8, LANES), 1)
    slots = sorted(s for s, _, _ in slot_of())
    pivots = sorted(slots + [CONST_SLOT])
    active = {32 * j + s for j in range(SPATIAL_TERMS) for s in slots}
    active |= {32 * j + CONST_SLOT for j in range(3)}

    def any_of(ids, chosen):
        mask = jnp.zeros(ids.shape, jnp.bool_)
        for c in chosen:
            mask = mask | (ids == c)
        return mask

    lanes_left = any_of(lane_id, sorted(u for u in active if u < LANES) + [SCIENCE_LANE])
    lanes_right = any_of(lane_id, [u - LANES for u in sorted(active) if u >= LANES])
    left, right = [], []
    total = jnp.zeros((8, LANES), jnp.float32)
    diagonals = []
    blocks = packed_blocks()
    packed = [gram_ref[8 * i : 8 * i + 8, :] for i in range(PACKED_ROWS // 8)]

    def gathered(i, columns):
        own = POWERS[i // 4]
        out = None
        for place, column in enumerate(columns):
            row, lane = blocks[(own[0] + POWERS[column][0], own[1] + POWERS[column][1])]
            source = packed[4 * row + i % 4]
            if place != lane:
                source = pltpu.roll(source, (SLOTS * (place - lane)) % LANES, 1)
            out = source if out is None else jnp.where(lane_id >= SLOTS * place, source, out)
        return out

    for i in range(24):
        rows = any_of(row_id, [u - 8 * i for u in sorted(active) if u // 8 == i])
        whole = packed[4 * (i // 4 - 2) + i % 4] if i >= 8 else gathered(i, (0, 1, 2, 3))
        a = jnp.where(rows & lanes_left, whole, 0.0)
        b = jnp.where(rows & lanes_right, gathered(i, (4, 5)), 0.0)
        diagonal = lane_id == (row_id + 8 * i) % LANES
        total = total + jnp.where(diagonal & rows, a if i < 16 else b, 0.0)
        left.append(a)
        right.append(b)
        diagonals.append((diagonal, rows))
    ridge = jnp.sum(total, axis=(0, 1), keepdims=True) * (RIDGE / UNKNOWNS)
    for i, (diagonal, rows) in enumerate(diagonals):
        added = jnp.where(diagonal, jnp.where(rows, ridge, 1.0), 0.0)
        if i < 16:
            left[i] = left[i] + jnp.where(lane_id == SCIENCE_LANE, 0.0, added)
        else:
            right[i] = right[i] + added

    def eliminate(left, right, high):
        left, right = list(left), list(right)
        columns = jnp.concatenate((right if high else left)[4:], axis=0)
        own = [left[:4], right[:4]] if high else [left[:4]]
        lead = len(own) - 1
        pairs = list(zip(pivots[0::2], pivots[1::2]))
        columns_p, columns_q = (spread_column(own[lead], c) for c in pairs[0])
        for step, (p, q) in enumerate(pairs):
            ahead = [(c, spread_column(own[lead], c)) for c in (pairs[step + 1] if step + 1 < len(pairs) else ())]
            pp, pq = row_spread(columns_p, p), row_spread(columns_q, p)
            qp, qq = row_spread(columns_p, q), row_spread(columns_q, q)
            scale = 1.0 / (pp * qq - pq * qp)

            def advance(tiles):
                row_p, row_q = row_spread(tiles, p), row_spread(tiles, q)
                new_p = (qq * row_p - pq * row_q) * scale
                new_q = (pp * row_q - qp * row_p) * scale
                out = []
                for i in range(4):
                    value = tiles[i] - columns_p[i] * new_p - columns_q[i] * new_q
                    if i == p // 8:
                        value = jnp.where(row_id == p % 8, new_p, value)
                    if i == q // 8:
                        value = jnp.where(row_id == q % 8, new_q, value)
                    out.append(value)
                return out

            following = [advance(tiles) for _, tiles in ahead]
            own = [advance(side) for side in own]
            if following:
                columns_p, columns_q = following
        rows = jnp.concatenate([jnp.concatenate(side, axis=0) for side in own], axis=1)
        rows = jnp.concatenate([rows, jnp.zeros((LANES - SLOTS, rows.shape[1]), jnp.float32)], axis=0)
        change = jnp.dot(
            columns, rows, precision=lax.Precision.HIGHEST, preferred_element_type=jnp.float32
        )
        for i in range(20):
            part = change[8 * i : 8 * i + 8]
            left[4 + i] = left[4 + i] - part[:, 0:LANES]
            if high:
                right[4 + i] = right[4 + i] - part[:, LANES:]
        left = left[4:] + own[0]
        if high:
            right = [pltpu.roll(v, LANES - SLOTS, 1) for v in right[4:] + own[1]]
        else:
            left = [pltpu.roll(v, LANES - SLOTS, 1) for v in left]
        return tuple(left), tuple(right)

    left, right = left[16:] + left[:16], right[16:] + right[:16]

    def both_sides(step, carry):
        beside(step)
        return eliminate(carry[0], carry[1], True)

    def left_side(step, carry):
        beside(2 * step + 2)
        beside(2 * step + 3)
        for f in range(3 * step, min(3 * step + 3, 11)):
            first_block(f)
        return eliminate(carry, (), False)[0]

    left, right = lax.fori_loop(0, 2, both_sides, (tuple(left), tuple(right)))
    for step in range(4):
        left = left_side(step, left)
    left = left[8:] + left[:8]
    return [lane_spread(v, SCIENCE_LANE) for v in left]


def model_kernel(row_ref, gram_ref, window_ref, down_ref, science_ref, *refs):
    across_refs = refs[0:3]
    out_ref = refs[3]
    vert_ref, a_buf, b_buf, c_buf, basis_even, basis_odd = refs[4:10]

    def filter_down(step):
        pair = jnp.minimum(step, TILE_COUNT // 2 - 1)
        columns = pl.ds(pl.multiple_of(pair * 2 * LANES, 2 * LANES), 2 * LANES)
        for block in range(STRIP_ROWS // STAMP_SIZE):
            rows = slice(block * STAMP_SIZE, block * STAMP_SIZE + PATCH)
            piece = jnp.concatenate([window_ref[2 * pair, rows, :], window_ref[2 * pair + 1, rows, :]], axis=1)
            high = piece.astype(jnp.bfloat16)
            low = (piece - high.astype(jnp.float32)).astype(jnp.bfloat16)
            stacked = jnp.concatenate([high, low, high], axis=0)
            out = jnp.dot(down_ref[...], stacked, preferred_element_type=jnp.float32)
            vert_ref[:, block * STAMP_SIZE : (block + 1) * STAMP_SIZE, columns] = out.astype(
                jnp.bfloat16
            ).reshape(11, STAMP_SIZE, 2 * LANES)

    slots = slot_of()
    group_first = (G0, G1, G2)

    def filter_block(pair, f, basis):
        g = 0 if f < 5 else (1 if f < 8 else 2)
        members = [(s, m) for s, ff, m in slots if ff == f]
        start = pl.multiple_of(pair * 2 * LANES, 2 * LANES)
        first = vert_ref[f, :, pl.ds(start, 2 * LANES)]
        second = vert_ref[f, :, pl.ds(pl.multiple_of(start + LANES, LANES), 2 * LANES)]
        out = jnp.dot(
            jnp.concatenate([first, second], axis=0),
            across_refs[g][:, 0 : len(members) * LANES],
            preferred_element_type=jnp.float32,
        )
        for s, m in members:
            k = m - group_first[g]
            basis[s, :, :] = out[:, k * LANES : (k + 1) * LANES]

    solution_tiles = solve(gram_ref, filter_down, lambda f: filter_block(0, f, basis_even))
    lane_id = lax.broadcasted_iota(jnp.int32, (8, LANES), 1)
    row_id = lax.broadcasted_iota(jnp.int32, (8, LANES), 0)
    blocks = COLUMNS // LANES
    quarters = STRIP_ROWS // 8
    base = row_ref[0]
    for i in range(blocks):
        x = (2.0 * (lane_id + i * LANES).astype(jnp.float32) + 1.0 - COLUMNS) / COLUMNS
        for t in range(4):
            c = [solution_tiles[4 * j + t] for j in range(SPATIAL_TERMS)]
            a_buf[i, 8 * t : 8 * t + 8, :] = c[AT_ONE] + x * (c[AT_X] + x * c[AT_XX])
            b_buf[i, 8 * t : 8 * t + 8, :] = c[AT_Y] + x * c[AT_XY]
    def row_position(q):
        return (2.0 * (row_id + 8 * q + base).astype(jnp.float32) + 1.0 - IMAGE_ROWS) / IMAGE_ROWS

    for q in range(quarters):
        y = row_position(q)
        for s, _, _ in slots:
            curve = jnp.broadcast_to(solution_tiles[4 * AT_YY + s // 8][s % 8 : s % 8 + 1, :], (8, LANES))
            c_buf[s, 8 * q : 8 * q + 8, :] = y * curve

    def combine(block, half, basis, origin):
        position = [row_position(q) for q in range(quarters)]
        flat = jnp.broadcast_to(a_buf[block, CONST_SLOT : CONST_SLOT + 1, :], (8, LANES))
        slope = jnp.broadcast_to(b_buf[block, CONST_SLOT : CONST_SLOT + 1, :], (8, LANES))
        total = [flat + y * slope for y in position]
        for s, _, _ in slots:
            flat = jnp.broadcast_to(a_buf[block, s : s + 1, :], (8, LANES))
            slope = jnp.broadcast_to(b_buf[block, s : s + 1, :], (8, LANES))
            for q in range(quarters):
                curve = c_buf[origin + s, 8 * q : 8 * q + 8, :]
                field = flat + position[q] * (slope + curve)
                at = STRIP_ROWS * half + 8 * q
                total[q] = total[q] + basis[s, at : at + 8, :] * field
            yield
        columns = pl.ds(pl.multiple_of(block * LANES, LANES), LANES)
        for q in range(quarters):
            rows = slice(8 * q, 8 * q + 8)
            out_ref[rows, columns] = science_ref[rows, columns] - total[q]

    @pl.loop(0, blocks // 4)
    def _(step):
        for n, (here, there) in enumerate(((basis_even, basis_odd), (basis_odd, basis_even))):
            pair = 2 * step + n
            following = jnp.minimum(pair + 1, blocks // 2 - 1)
            steps = itertools.chain(
                *(combine(2 * pair + half, half, here, row_ref[1 + 2 * n + half]) for half in range(2))
            )
            for f in range(11):
                filter_block(following, f, there)
                for _ in range(5):
                    next(steps, None)
            for _ in steps:
                pass


def place(z, x, y):
    return (z % 2) * 16 + (x % 4) * 4 + y % 4


def shift(dz, dx, dy):
    return [(place(z, x, y), place(z + dz, x + dx, y + dy)) for z in range(2) for x in range(4) for y in range(4)]


def gather_template(piece):
    def move(value, *step):
        return lax.ppermute(value, "exp", shift(*step))

    def paired(value, axis, partner):
        def other(z, x, y):
            return place(z, partner(x), y) if axis == "x" else place(z, x, partner(y))

        pairs = [(place(z, x, y), other(z, x, y)) for z in range(2) for x in range(4) for y in range(4)]
        return lax.ppermute(value, "exp", pairs)

    def doubled(value, axis):
        near = lax.optimization_barrier(jnp.stack([value, paired(value, axis, lambda i: i ^ 1)]))
        far = paired(near, axis, lambda i: 3 - i)
        return lax.optimization_barrier(jnp.concatenate([near, far]))

    along_x = ((0, 1, 0), (0, -1, 0), (0, 2, 0))
    along_y = ((0, 0, 1), (0, 0, -1), (0, 0, 2))
    other = move(piece, 1, 0, 0)
    both = lax.optimization_barrier(jnp.stack([piece, other]))
    part_a = doubled(both[:, :PIECE_A], "y")
    part_b = doubled(both[:, PIECE_A:], "x")
    parts_a = [part_a] + [move(part_a, *s) for s in along_x]
    parts_b = [part_b] + [move(part_b, *s) for s in along_y]
    return parts_a, parts_b


def reduce_strips(value):
    value = value + lax.ppermute(value, "strip", [(0, 1), (1, 0), (2, 3), (3, 2)])
    return value + lax.ppermute(value, "strip", [(0, 2), (2, 0), (1, 3), (3, 1)])


VMEM = pltpu.MemorySpace.VMEM
SMEM = pltpu.MemorySpace.SMEM


def kept(value):
    return pltpu.with_memory_space_constraint(value, VMEM)


def vmem():
    return pl.BlockSpec(memory_space=VMEM)


def smem():
    return pl.BlockSpec(memory_space=SMEM)


def shards(science, variance, template, offset_rows, offset_cols, stamp_rows, stamp_cols):
    strip_index = lax.axis_index("strip")
    place = lax.axis_index("exp")
    row_base = (strip_index * STRIP_ROWS).astype(jnp.int32)
    picture = kept(science[0])
    piece = pl.pallas_call(
        pack_kernel,
        out_shape=pltpu.VMEM((PIECE_A + PIECE_B, LANES), jnp.float32),
        in_specs=[smem(), vmem()],
        out_specs=vmem(),
        name="pack",
    )(strip_index.astype(jnp.int32)[None], template.T)
    parts_a, parts_b = gather_template(piece)
    scalars = jnp.stack([place.astype(jnp.int32), offset_rows[0], offset_cols[0], row_base])
    gram, window = pl.pallas_call(
        stamps_kernel,
        out_shape=(
            pltpu.VMEM((PACKED_ROWS, LANES), jnp.float32),
            pltpu.VMEM((TILE_COUNT, WINDOW, LANES), jnp.float32),
        ),
        in_specs=[smem()] * 3 + [vmem()] * 9 + [pl.BlockSpec(memory_space=pl.ANY)] + [vmem()] * 2,
        out_specs=(vmem(), vmem()),
        scratch_shapes=[
            pltpu.VMEM((WIDE + 2 * LANES, LANES), jnp.float32),
            pltpu.VMEM((WIDE + 2 * LANES, LANES), jnp.float32),
            pltpu.VMEM((TILE_COUNT, NEED_ROWS + 8, LANES), jnp.float32),
            pltpu.VMEM((3 * PATCH, STAMP_COUNT * LANES), jnp.bfloat16),
            pltpu.VMEM((1024, 4 * LANES), jnp.bfloat16),
            pltpu.VMEM((4, 2, CUT_ROWS, LANES), jnp.float32),
            pltpu.VMEM((STAMP_SIZE, LANES), jnp.float32),
            pltpu.VMEM((STAMP_SIZE, LANES), jnp.float32),
            pltpu.VMEM((4, STAMP_SIZE, 8, LANES), jnp.float32),
            pltpu.VMEM((PADDED, STAMP_COUNT * STAMP_SIZE * STAMP_SIZE), jnp.bfloat16),
            pltpu.VMEM((4 * LANES, ACROSS_COUNT * LANES), jnp.bfloat16),
            pltpu.VMEM((STRIP_ROWS, COLUMNS), jnp.float32),
            pltpu.SemaphoreType.DMA,
        ],
        compiler_params=pltpu.CompilerParams(vmem_limit_bytes=28 << 20),
        name="stamps",
    )(
        scalars,
        stamp_rows[0],
        stamp_cols[0],
        *[kept(part) for part in parts_a + parts_b],
        picture,
        variance[0],
        kept(jnp.asarray(stamp_down())),
        kept(jnp.asarray(stamp_across())),
    )
    total = reduce_strips(gram)
    band = across_band(LANES)
    bands = [
        kept(jnp.asarray(band[:, first : first + degree + 1].reshape(2 * LANES, -1)))
        for first, degree in zip((G0, G1, G2), DEGREES)
    ]
    result = pl.pallas_call(
        model_kernel,
        out_shape=jax.ShapeDtypeStruct((STRIP_ROWS, COLUMNS), jnp.float32),
        in_specs=[smem()] + [vmem()] * 7,
        out_specs=vmem(),
        scratch_shapes=[
            pltpu.VMEM((11, STRIP_ROWS, TILE_COUNT * LANES), jnp.bfloat16),
            pltpu.VMEM((COLUMNS // LANES, SLOTS, LANES), jnp.float32),
            pltpu.VMEM((COLUMNS // LANES, SLOTS, LANES), jnp.float32),
            pltpu.VMEM((SLOTS, STRIP_ROWS, LANES), jnp.float32),
            pltpu.VMEM((SLOTS, 2 * STRIP_ROWS, LANES), jnp.float32),
            pltpu.VMEM((SLOTS, 2 * STRIP_ROWS, LANES), jnp.float32),
        ],
        compiler_params=pltpu.CompilerParams(vmem_limit_bytes=32 << 20),
        name="model",
    )(jnp.stack([row_base] + [row_base * 0] * 4), kept(total), window, kept(jnp.asarray(full_down())), picture, *bands)
    return result[None]


def solution(mesh):
    in_specs = (
        P("exp", "strip", None),
        P("exp", "strip", None),
        P(None, "exp"),
        P("exp"),
        P("exp"),
        P("exp", "strip"),
        P("exp", "strip"),
    )
    out_specs = P("exp", "strip", None)
    return jax.shard_map(shards, mesh=mesh, in_specs=in_specs, out_specs=out_specs, check_vma=False)
```

```python
import itertools

import jax
import jax.numpy as jnp
import ml_dtypes
import numpy as np
from jax import lax
from jax.experimental import pallas as pl
from jax.experimental.pallas import tpu as pltpu
from jax.sharding import PartitionSpec as P

STRIP_ROWS = 128
COLUMNS = 2048
IMAGE_ROWS = 512
STAMP_COUNT = 16
STAMP_SIZE = 32
SPATIAL_TERMS = 6
KERNEL_HALF = 20
UNKNOWNS = 165
RIDGE = 0.001
SIGMAS = (1.0, 2.0, 4.0)
DEGREES = (4, 2, 2)

LANES = 128
SOURCE_COLS = 68
NEED_ROWS = 192
WIDE = 2176
TILE_COUNT = 18
PATCH = 80
WINDOW = 176
CUT_ROWS = 40
PIECE_A = 56
PIECE_B = 48

G0, G1, G2 = 0, 5, 8
TILES = (
    ((G0 + 0, (0, 1, 2, 3, 4)), (G0 + 2, (0, 1, 2))),
    ((G0 + 1, (0, 1, 2, 3)), (G0 + 3, (0, 1)), (G0 + 4, (0,))),
    ((G1 + 0, (5, 6, 7)), (G1 + 1, (5, 6)), (G1 + 2, (5,))),
    ((G2 + 0, (8, 9, 10)), (G2 + 1, (8, 9)), (G2 + 2, (8,))),
)
CONST_SLOT = 15
SCIENCE_SLOT = 22
SLOTS = 32
PADDED = SPATIAL_TERMS * SLOTS
POWERS = ((1, 0), (0, 1), (0, 0), (2, 0), (0, 2), (1, 1))
AT_X, AT_Y, AT_ONE, AT_XX, AT_YY, AT_XY = range(SPATIAL_TERMS)
SCIENCE_LANE = SLOTS * AT_ONE + SCIENCE_SLOT
PACKED_ROWS = 5 * SLOTS


def packed_blocks():
    blocks = {}
    for r, left in enumerate(POWERS[2:]):
        for c, right in enumerate(POWERS[:4]):
            blocks.setdefault((left[0] + right[0], left[1] + right[1]), (r, c))
    blocks[(1, 3)] = (4, 0)
    blocks[(0, 4)] = (4, 1)
    return blocks


def tap_table():
    offsets = np.arange(-KERNEL_HALF, KERNEL_HALF + 1).astype(np.float64)
    entries = []
    for spread, degree in zip(SIGMAS, DEGREES):
        profile = np.exp(-offsets * offsets / (2.0 * spread * spread))
        profile = profile / profile.sum()
        for exponent in range(degree + 1):
            entries.append((offsets / spread) ** exponent * profile)
    table = np.stack(entries)
    table[np.abs(table) < 1.2e-38] = 0.0
    return table.astype(np.float32)


def split_halves(table):
    high = table.astype(ml_dtypes.bfloat16)
    low = (table - high.astype(np.float32)).astype(ml_dtypes.bfloat16)
    return high, low


def down_rows(filters, rows):
    taps = tap_table()
    full = np.zeros((len(filters), rows, PATCH), np.float32)
    for i, f in enumerate(filters):
        if f is not None:
            for r in range(rows):
                full[i, r, r : r + 2 * KERNEL_HALF + 1] = taps[f]
    high, low = split_halves(full)
    return np.concatenate([high, high, low], axis=2)


def stamp_down():
    blocks = []
    for tile in TILES:
        filters = [f for _, down in tile for f in down]
        filters += [None] * (8 - len(filters))
        blocks.append(down_rows(filters, STAMP_SIZE).transpose(1, 0, 2).reshape(-1, 3 * PATCH))
    return np.concatenate(blocks)


def full_down():
    return down_rows(list(range(11)), STAMP_SIZE).reshape(-1, 3 * PATCH)


def across_band(width):
    short = tap_table().astype(ml_dtypes.bfloat16)
    band = np.zeros((2 * LANES, 11, width), ml_dtypes.bfloat16)
    for m in range(11):
        for c in range(width):
            band[c : c + 2 * KERNEL_HALF + 1, m, c] = short[m]
    return band


def stamp_across():
    band = across_band(STAMP_SIZE)[:LANES]
    return np.concatenate([np.tile(band[:, m], (1, 4)) for tile in TILES for m, _ in tile], axis=1)


ACROSS_COUNT = sum(len(tile) for tile in TILES)


def slot_of():
    slots = []
    for t, tile in enumerate(TILES):
        s = 8 * t
        for across, down in tile:
            for f in down:
                slots.append((s, f, across))
                s += 1
    return slots


def pack_kernel(strip_ref, template_ref, piece_ref):
    start = pl.multiple_of(strip_ref[0] * LANES, LANES)
    first = template_ref[:, pl.ds(start, LANES)]
    second = template_ref[:, pl.ds(start + LANES, NEED_ROWS - LANES)]
    half = SOURCE_COLS // 2
    piece_ref[0:PIECE_A, :] = first[:PIECE_A]
    piece_ref[PIECE_A + PIECE_B - 8 :, :] = jnp.zeros((8, LANES), jnp.float32)
    piece_ref[PIECE_A : PIECE_A + half, 0:64] = second[:half]
    piece_ref[PIECE_A : PIECE_A + half, 64:128] = second[half:]
    piece_ref[PIECE_A + half : half + SOURCE_COLS, :] = first[PIECE_A:]


def stamps_kernel(scalars, rows_ref, cols_ref, *refs):
    a_refs = refs[0:4]
    b_refs = refs[4:8]
    science_ref, variance_ref, down_hbm, across_hbm = refs[8:12]
    gram_ref, window_ref = refs[12:14]
    t_one, t_two, w_buf, patches, vert, cut_buf, sci_buf, wt_buf, bases, design, across_buf = refs[14:25]
    variance_buf, down_ref, across_ref, sums, copied = refs[25:]
    copies = (
        pltpu.make_async_copy(down_hbm, down_ref, copied.at[0]),
        pltpu.make_async_copy(across_hbm, across_ref, copied.at[1]),
        pltpu.make_async_copy(variance_ref, variance_buf, copied.at[2]),
    )
    for copy in copies:
        copy.start()
    place, shift_down, shift_side, row_base = scalars[0], scalars[1], scalars[2], scalars[3]
    my_z, my_x, my_y = place // 16, (place // 4) % 4, place % 4
    half = SOURCE_COLS // 2
    def direct(own):
        return (own, (own + 3) % 4, (own + 1) % 4, (own + 2) % 4)

    def doubled(own):
        near = own + 1 - 2 * (own % 2)
        return (own, near, 3 - own, 3 - near)

    for first in range(4):
        for second in range(4):
            for dz in range(2):
                for is_a in (True, False):
                    along_x = direct(my_x)[first] if is_a else doubled(my_x)[second]
                    along_y = doubled(my_y)[second] if is_a else direct(my_y)[first]
                    source = ((my_z + dz) % 2) * 16 + along_x * 4 + along_y
                    base = source * SOURCE_COLS
                    if is_a:
                        t_one[pl.ds(base, PIECE_A), :] = a_refs[first][second, dz]
                    else:
                        rest = b_refs[first][second, dz, 0:half, :]
                        t_two[pl.ds(base, half), :] = rest
                        t_two[pl.ds(base + half, half), :] = pltpu.roll(rest, 64, 1)
                        t_one[pl.ds(base + PIECE_A, SOURCE_COLS - PIECE_A), :] = b_refs[first][
                            second, dz, half : half + SOURCE_COLS - PIECE_A, :
                        ]
    t_one[pl.ds(WIDE, 2 * LANES), :] = jnp.zeros((2 * LANES, LANES), jnp.float32)
    t_two[pl.ds(WIDE, 2 * LANES), :] = jnp.zeros((2 * LANES, LANES), jnp.float32)
    w_buf[:, NEED_ROWS:, :] = jnp.zeros((TILE_COUNT, 8, LANES), jnp.float32)

    @pl.loop(0, TILE_COUNT)
    def _(i):
        w_buf[i, 0:LANES, :] = t_one[pl.ds(shift_side + i * LANES, LANES), :].T
        w_buf[i, LANES:NEED_ROWS, :] = t_two[pl.ds(shift_side + i * LANES, LANES), :].T[
            0 : NEED_ROWS - LANES
        ]
        window_ref[i, :, :] = w_buf[i, pl.ds(shift_down, WINDOW), :]

    lane = lax.broadcasted_iota(jnp.int32, (1, LANES), 1)

    @pl.loop(0, STAMP_COUNT)
    def _(s):
        top, left = rows_ref[s], cols_ref[s]
        tile = left // LANES
        rest = left % LANES
        back = (LANES - rest) % LANES
        low = pltpu.roll(window_ref[tile, pl.ds(top, PATCH), :], back, 1)
        high = pltpu.roll(window_ref[tile + 1, pl.ds(top, PATCH), :], back, 1)
        patch = jnp.where(lane < LANES - rest, low, high)
        patch_high = patch.astype(jnp.bfloat16)
        patch_low = (patch - patch_high.astype(jnp.float32)).astype(jnp.bfloat16)
        here = pl.ds(pl.multiple_of(s * LANES, LANES), LANES)
        patches[0:PATCH, here] = patch_high
        patches[PATCH : 2 * PATCH, here] = patch_low
        patches[2 * PATCH :, here] = patch_high

    for copy in copies:
        copy.wait()
    slot = lax.broadcasted_iota(jnp.int32, (8, LANES), 0)
    for member in range(4):
        own = ((lane >= STAMP_SIZE * member) & (lane < STAMP_SIZE * (member + 1))).astype(jnp.bfloat16)
        for n in range(ACROSS_COUNT):
            here = slice(n * LANES, (n + 1) * LANES)
            across_buf[member * LANES : (member + 1) * LANES, here] = across_ref[:, here] * own

    sums[...] = jnp.zeros_like(sums)

    def add_products(at):
        sums[:, 0 : PADDED - SLOTS] += lax.dot_general(
            design[at, PADDED - LANES :, :],
            design[at, 0 : PADDED - SLOTS, :],
            (((1,), (1,)), ((), ())),
            preferred_element_type=jnp.float32,
        )

    @pl.loop(0, STAMP_COUNT // 4)
    def _(group):
        science = jnp.zeros((STAMP_SIZE, LANES), jnp.float32)
        noise = jnp.ones((STAMP_SIZE, LANES), jnp.float32)
        x_row = jnp.zeros((1, LANES), jnp.float32)
        y_row = jnp.zeros((1, LANES), jnp.float32)
        for member in range(4):
            s = 4 * group + member
            top, left = rows_ref[s], cols_ref[s]
            tile = left // LANES
            tile_start = pl.multiple_of(tile * LANES, LANES)
            next_start = pl.multiple_of(jnp.minimum(tile + 1, COLUMNS // LANES - 1) * LANES, LANES)
            rest = left % LANES
            turn = (LANES + STAMP_SIZE * member - rest) % LANES
            inside = (lane >= STAMP_SIZE * member) & (lane < STAMP_SIZE * (member + 1))
            from_low = lane - STAMP_SIZE * member + rest < LANES
            row_start = pl.multiple_of(jnp.minimum((top // 8) * 8, STRIP_ROWS - CUT_ROWS), 8)
            row_rest = top - row_start
            pieces = []
            for n, ref in enumerate((science_ref, variance_buf)):
                low = pltpu.roll(ref[pl.ds(row_start, CUT_ROWS), pl.ds(tile_start, LANES)], turn, 1)
                high = pltpu.roll(ref[pl.ds(row_start, CUT_ROWS), pl.ds(next_start, LANES)], turn, 1)
                cut_buf[member, n, :, :] = jnp.where(from_low, low, high)
                pieces.append(cut_buf[member, n, pl.ds(row_rest, STAMP_SIZE), :])
            science = jnp.where(inside, pieces[0], science)
            noise = jnp.where(inside, pieces[1], noise)
            col = (left + lane - STAMP_SIZE * member).astype(jnp.float32)
            row = (row_base + top + jnp.zeros_like(lane)).astype(jnp.float32)
            x_row = jnp.where(inside, (2.0 * col + 1.0 - COLUMNS) / COLUMNS, x_row)
            y_row = jnp.where(inside, (2.0 * row + 1.0 - IMAGE_ROWS) / IMAGE_ROWS, y_row)
        sci_buf[...] = science
        wt_buf[...] = lax.rsqrt(noise)
        x = jnp.broadcast_to(x_row, (8, LANES))
        y_first = jnp.broadcast_to(y_row, (8, LANES))
        vert[...] = jnp.dot(
            down_ref[...],
            patches[:, pl.ds(pl.multiple_of(group * 4 * LANES, 4 * LANES), 4 * LANES)],
            preferred_element_type=jnp.float32,
        ).astype(jnp.bfloat16)
        column = 0
        for t, tile in enumerate(TILES):
            out = jnp.dot(
                vert[t * 256 : (t + 1) * 256, :],
                across_buf[:, column : column + len(tile) * LANES],
                preferred_element_type=jnp.float32,
            )
            column += len(tile) * LANES
            out = out.reshape(STAMP_SIZE, 8, len(tile) * LANES)
            value = out[:, :, 0:LANES]
            edge = len(tile[0][1])
            for i in range(1, len(tile)):
                value = jnp.where(slot[None] >= edge, out[:, :, i * LANES : (i + 1) * LANES], value)
                edge += len(tile[i][1])
            if t == CONST_SLOT // 8:
                value = jnp.where(slot[None] == CONST_SLOT % 8, 1.0, value)
            bases[t, :, :, :] = value

        for r in range(STAMP_SIZE):
            science = jnp.broadcast_to(sci_buf[r : r + 1, :], (8, LANES))
            weight = jnp.broadcast_to(wt_buf[r : r + 1, :], (8, LANES))
            tiles = [bases[t, r] for t in range(4)]
            tiles[SCIENCE_SLOT // 8] = jnp.where(
                slot == SCIENCE_SLOT % 8, science, tiles[SCIENCE_SLOT // 8]
            )
            y = y_first + 2.0 * r / IMAGE_ROWS
            tiles = [b * weight for b in tiles]
            terms = (x, y, None, x * x, y * y, x * y)
            for j, term in enumerate(terms):
                values = tiles if term is None else [b * term for b in tiles]
                design[group + 1, j * SLOTS : (j + 1) * SLOTS, r * LANES : (r + 1) * LANES] = jnp.concatenate(
                    values, axis=0
                ).astype(jnp.bfloat16)

    for at in range(1, STAMP_COUNT // 4 + 1):
        add_products(at)
    gram_ref[0:LANES, :] = sums[:, 0:LANES]
    left = sums[LANES - SLOTS :, LANES:]
    right = pltpu.roll(sums[LANES - 2 * SLOTS : LANES - SLOTS, LANES:], SLOTS, 1)
    gram_ref[LANES:, :] = jnp.where(lane < SLOTS, left, right)


def lane_spread(value, index):
    return jnp.take_along_axis(value, jnp.full((8, LANES), index, jnp.int32), axis=1)


def spread_column(tiles, index):
    return [lane_spread(v, index) for v in tiles]


def row_spread(tiles, index):
    return jnp.broadcast_to(tiles[index // 8][index % 8 : index % 8 + 1, :], (8, LANES))


def solve(gram_ref, beside, first_block):
    row_id = lax.broadcasted_iota(jnp.int32, (8, LANES), 0)
    lane_id = lax.broadcasted_iota(jnp.int32, (8, LANES), 1)
    slots = sorted(s for s, _, _ in slot_of())
    pivots = sorted(slots + [CONST_SLOT])
    active = {32 * j + s for j in range(SPATIAL_TERMS) for s in slots}
    active |= {32 * j + CONST_SLOT for j in range(3)}

    def any_of(ids, chosen):
        mask = jnp.zeros(ids.shape, jnp.bool_)
        for c in chosen:
            mask = mask | (ids == c)
        return mask

    lanes_left = any_of(lane_id, sorted(u for u in active if u < LANES) + [SCIENCE_LANE])
    lanes_right = any_of(lane_id, [u - LANES for u in sorted(active) if u >= LANES])
    left, right = [], []
    total = jnp.zeros((8, LANES), jnp.float32)
    diagonals = []
    blocks = packed_blocks()
    packed = [gram_ref[8 * i : 8 * i + 8, :] for i in range(PACKED_ROWS // 8)]

    def gathered(i, columns):
        own = POWERS[i // 4]
        out = None
        for place, column in enumerate(columns):
            row, lane = blocks[(own[0] + POWERS[column][0], own[1] + POWERS[column][1])]
            source = packed[4 * row + i % 4]
            if place != lane:
                source = pltpu.roll(source, (SLOTS * (place - lane)) % LANES, 1)
            out = source if out is None else jnp.where(lane_id >= SLOTS * place, source, out)
        return out

    for i in range(24):
        rows = any_of(row_id, [u - 8 * i for u in sorted(active) if u // 8 == i])
        whole = packed[4 * (i // 4 - 2) + i % 4] if i >= 8 else gathered(i, (0, 1, 2, 3))
        a = jnp.where(rows & lanes_left, whole, 0.0)
        b = jnp.where(rows & lanes_right, gathered(i, (4, 5)), 0.0)
        diagonal = lane_id == (row_id + 8 * i) % LANES
        total = total + jnp.where(diagonal & rows, a if i < 16 else b, 0.0)
        left.append(a)
        right.append(b)
        diagonals.append((diagonal, rows))
    ridge = jnp.sum(total, axis=(0, 1), keepdims=True) * (RIDGE / UNKNOWNS)
    for i, (diagonal, rows) in enumerate(diagonals):
        added = jnp.where(diagonal, jnp.where(rows, ridge, 1.0), 0.0)
        if i < 16:
            left[i] = left[i] + jnp.where(lane_id == SCIENCE_LANE, 0.0, added)
        else:
            right[i] = right[i] + added

    def eliminate(left, right, high):
        left, right = list(left), list(right)
        columns = jnp.concatenate((right if high else left)[4:], axis=0)
        own = [left[:4], right[:4]] if high else [left[:4]]
        lead = len(own) - 1
        pairs = list(zip(pivots[0::2], pivots[1::2]))
        columns_p, columns_q = (spread_column(own[lead], c) for c in pairs[0])
        for step, (p, q) in enumerate(pairs):
            ahead = [(c, spread_column(own[lead], c)) for c in (pairs[step + 1] if step + 1 < len(pairs) else ())]
            pp, pq = row_spread(columns_p, p), row_spread(columns_q, p)
            qp, qq = row_spread(columns_p, q), row_spread(columns_q, q)
            scale = 1.0 / (pp * qq - pq * qp)

            def advance(tiles):
                row_p, row_q = row_spread(tiles, p), row_spread(tiles, q)
                new_p = (qq * row_p - pq * row_q) * scale
                new_q = (pp * row_q - qp * row_p) * scale
                out = []
                for i in range(4):
                    value = tiles[i] - columns_p[i] * new_p - columns_q[i] * new_q
                    if i == p // 8:
                        value = jnp.where(row_id == p % 8, new_p, value)
                    if i == q // 8:
                        value = jnp.where(row_id == q % 8, new_q, value)
                    out.append(value)
                return out

            following = [advance(tiles) for _, tiles in ahead]
            own = [advance(side) for side in own]
            if following:
                columns_p, columns_q = following
        rows = jnp.concatenate([jnp.concatenate(side, axis=0) for side in own], axis=1)
        rows = jnp.concatenate([rows, jnp.zeros((LANES - SLOTS, rows.shape[1]), jnp.float32)], axis=0)
        change = jnp.dot(
            columns, rows, precision=lax.Precision.HIGHEST, preferred_element_type=jnp.float32
        )
        for i in range(20):
            part = change[8 * i : 8 * i + 8]
            left[4 + i] = left[4 + i] - part[:, 0:LANES]
            if high:
                right[4 + i] = right[4 + i] - part[:, LANES:]
        left = left[4:] + own[0]
        if high:
            right = [pltpu.roll(v, LANES - SLOTS, 1) for v in right[4:] + own[1]]
        else:
            left = [pltpu.roll(v, LANES - SLOTS, 1) for v in left]
        return tuple(left), tuple(right)

    left, right = left[16:] + left[:16], right[16:] + right[:16]

    def both_sides(step, carry):
        beside(step)
        return eliminate(carry[0], carry[1], True)

    def left_side(step, carry):
        beside(2 * step + 2)
        beside(2 * step + 3)
        for f in range(3 * step, min(3 * step + 3, 11)):
            first_block(f)
        return eliminate(carry, (), False)[0]

    left, right = lax.fori_loop(0, 2, both_sides, (tuple(left), tuple(right)))
    for step in range(4):
        left = left_side(step, left)
    left = left[8:] + left[:8]
    return [lane_spread(v, SCIENCE_LANE) for v in left]


def model_kernel(row_ref, gram_ref, window_ref, down_ref, science_ref, *refs):
    across_refs = refs[0:3]
    out_ref = refs[3]
    vert_ref, a_buf, b_buf, c_buf, basis_even, basis_odd = refs[4:10]

    def filter_down(step):
        pair = jnp.minimum(step, TILE_COUNT // 2 - 1)
        columns = pl.ds(pl.multiple_of(pair * 2 * LANES, 2 * LANES), 2 * LANES)
        for block in range(STRIP_ROWS // STAMP_SIZE):
            rows = slice(block * STAMP_SIZE, block * STAMP_SIZE + PATCH)
            piece = jnp.concatenate([window_ref[2 * pair, rows, :], window_ref[2 * pair + 1, rows, :]], axis=1)
            high = piece.astype(jnp.bfloat16)
            low = (piece - high.astype(jnp.float32)).astype(jnp.bfloat16)
            stacked = jnp.concatenate([high, low, high], axis=0)
            out = jnp.dot(down_ref[...], stacked, preferred_element_type=jnp.float32)
            vert_ref[:, block * STAMP_SIZE : (block + 1) * STAMP_SIZE, columns] = out.astype(
                jnp.bfloat16
            ).reshape(11, STAMP_SIZE, 2 * LANES)

    slots = slot_of()
    group_first = (G0, G1, G2)

    def filter_block(pair, f, basis):
        g = 0 if f < 5 else (1 if f < 8 else 2)
        members = [(s, m) for s, ff, m in slots if ff == f]
        start = pl.multiple_of(pair * 2 * LANES, 2 * LANES)
        first = vert_ref[f, :, pl.ds(start, 2 * LANES)]
        second = vert_ref[f, :, pl.ds(pl.multiple_of(start + LANES, LANES), 2 * LANES)]
        out = jnp.dot(
            jnp.concatenate([first, second], axis=0),
            across_refs[g][:, 0 : len(members) * LANES],
            preferred_element_type=jnp.float32,
        )
        for s, m in members:
            k = m - group_first[g]
            basis[s, :, :] = out[:, k * LANES : (k + 1) * LANES]

    solution_tiles = solve(gram_ref, filter_down, lambda f: filter_block(0, f, basis_even))
    lane_id = lax.broadcasted_iota(jnp.int32, (8, LANES), 1)
    row_id = lax.broadcasted_iota(jnp.int32, (8, LANES), 0)
    blocks = COLUMNS // LANES
    quarters = STRIP_ROWS // 8
    base = row_ref[0]
    for i in range(blocks):
        x = (2.0 * (lane_id + i * LANES).astype(jnp.float32) + 1.0 - COLUMNS) / COLUMNS
        for t in range(4):
            c = [solution_tiles[4 * j + t] for j in range(SPATIAL_TERMS)]
            a_buf[i, 8 * t : 8 * t + 8, :] = c[AT_ONE] + x * (c[AT_X] + x * c[AT_XX])
            b_buf[i, 8 * t : 8 * t + 8, :] = c[AT_Y] + x * c[AT_XY]
    def row_position(q):
        return (2.0 * (row_id + 8 * q + base).astype(jnp.float32) + 1.0 - IMAGE_ROWS) / IMAGE_ROWS

    for q in range(quarters):
        y = row_position(q)
        for s, _, _ in slots:
            curve = jnp.broadcast_to(solution_tiles[4 * AT_YY + s // 8][s % 8 : s % 8 + 1, :], (8, LANES))
            c_buf[s, 8 * q : 8 * q + 8, :] = y * curve

    def combine(block, half, basis, origin):
        position = [row_position(q) for q in range(quarters)]
        flat = jnp.broadcast_to(a_buf[block, CONST_SLOT : CONST_SLOT + 1, :], (8, LANES))
        slope = jnp.broadcast_to(b_buf[block, CONST_SLOT : CONST_SLOT + 1, :], (8, LANES))
        total = [flat + y * slope for y in position]
        for s, _, _ in slots:
            flat = jnp.broadcast_to(a_buf[block, s : s + 1, :], (8, LANES))
            slope = jnp.broadcast_to(b_buf[block, s : s + 1, :], (8, LANES))
            for q in range(quarters):
                curve = c_buf[origin + s, 8 * q : 8 * q + 8, :]
                field = flat + position[q] * (slope + curve)
                at = STRIP_ROWS * half + 8 * q
                total[q] = total[q] + basis[s, at : at + 8, :] * field
            yield
        columns = pl.ds(pl.multiple_of(block * LANES, LANES), LANES)
        for q in range(quarters):
            rows = slice(8 * q, 8 * q + 8)
            out_ref[rows, columns] = science_ref[rows, columns] - total[q]

    @pl.loop(0, blocks // 4)
    def _(step):
        for n, (here, there) in enumerate(((basis_even, basis_odd), (basis_odd, basis_even))):
            pair = 2 * step + n
            following = jnp.minimum(pair + 1, blocks // 2 - 1)
            steps = itertools.chain(
                *(combine(2 * pair + half, half, here, row_ref[1 + 2 * n + half]) for half in range(2))
            )
            for f in range(11):
                filter_block(following, f, there)
                for _ in range(5):
                    next(steps, None)
            for _ in steps:
                pass


def place(z, x, y):
    return (z % 2) * 16 + (x % 4) * 4 + y % 4


def shift(dz, dx, dy):
    return [(place(z, x, y), place(z + dz, x + dx, y + dy)) for z in range(2) for x in range(4) for y in range(4)]


def gather_template(piece):
    def move(value, *step):
        return lax.ppermute(value, "exp", shift(*step))

    def paired(value, axis, partner):
        def other(z, x, y):
            return place(z, partner(x), y) if axis == "x" else place(z, x, partner(y))

        pairs = [(place(z, x, y), other(z, x, y)) for z in range(2) for x in range(4) for y in range(4)]
        return lax.ppermute(value, "exp", pairs)

    def doubled(value, axis):
        near = lax.optimization_barrier(jnp.stack([value, paired(value, axis, lambda i: i ^ 1)]))
        far = paired(near, axis, lambda i: 3 - i)
        return lax.optimization_barrier(jnp.concatenate([near, far]))

    along_x = ((0, 1, 0), (0, -1, 0), (0, 2, 0))
    along_y = ((0, 0, 1), (0, 0, -1), (0, 0, 2))
    other = move(piece, 1, 0, 0)
    both = lax.optimization_barrier(jnp.stack([piece, other]))
    part_a = doubled(both[:, :PIECE_A], "y")
    part_b = doubled(both[:, PIECE_A:], "x")
    parts_a = [part_a] + [move(part_a, *s) for s in along_x]
    parts_b = [part_b] + [move(part_b, *s) for s in along_y]
    return parts_a, parts_b


def reduce_strips(value):
    value = value + lax.ppermute(value, "strip", [(0, 1), (1, 0), (2, 3), (3, 2)])
    return value + lax.ppermute(value, "strip", [(0, 2), (2, 0), (1, 3), (3, 1)])


VMEM = pltpu.MemorySpace.VMEM
SMEM = pltpu.MemorySpace.SMEM
HBM = pltpu.MemorySpace.HBM


def kept(value):
    return pltpu.with_memory_space_constraint(value, VMEM)


def vmem():
    return pl.BlockSpec(memory_space=VMEM)


def smem():
    return pl.BlockSpec(memory_space=SMEM)


def shards(science, variance, template, offset_rows, offset_cols, stamp_rows, stamp_cols):
    strip_index = lax.axis_index("strip")
    place = lax.axis_index("exp")
    row_base = (strip_index * STRIP_ROWS).astype(jnp.int32)
    picture = kept(science[0])
    piece = pl.pallas_call(
        pack_kernel,
        out_shape=pltpu.VMEM((PIECE_A + PIECE_B, LANES), jnp.float32),
        in_specs=[smem(), vmem()],
        out_specs=vmem(),
        name="pack",
    )(strip_index.astype(jnp.int32)[None], template.T)
    parts_a, parts_b = gather_template(piece)
    scalars = jnp.stack([place.astype(jnp.int32), offset_rows[0], offset_cols[0], row_base])
    gram, window = pl.pallas_call(
        stamps_kernel,
        out_shape=(
            pltpu.VMEM((PACKED_ROWS, LANES), jnp.float32),
            pltpu.VMEM((TILE_COUNT, WINDOW, LANES), jnp.float32),
        ),
        in_specs=[smem()] * 3 + [vmem()] * 9 + [pl.BlockSpec(memory_space=pl.ANY)] + [pl.BlockSpec(memory_space=HBM)] * 2,
        out_specs=(vmem(), vmem()),
        scratch_shapes=[
            pltpu.VMEM((WIDE + 2 * LANES, LANES), jnp.float32),
            pltpu.VMEM((WIDE + 2 * LANES, LANES), jnp.float32),
            pltpu.VMEM((TILE_COUNT, NEED_ROWS + 8, LANES), jnp.float32),
            pltpu.VMEM((3 * PATCH, STAMP_COUNT * LANES), jnp.bfloat16),
            pltpu.VMEM((1024, 4 * LANES), jnp.bfloat16),
            pltpu.VMEM((4, 2, CUT_ROWS, LANES), jnp.float32),
            pltpu.VMEM((STAMP_SIZE, LANES), jnp.float32),
            pltpu.VMEM((STAMP_SIZE, LANES), jnp.float32),
            pltpu.VMEM((4, STAMP_SIZE, 8, LANES), jnp.float32),
            pltpu.VMEM((STAMP_COUNT // 4 + 1, PADDED, STAMP_SIZE * LANES), jnp.bfloat16),
            pltpu.VMEM((4 * LANES, ACROSS_COUNT * LANES), jnp.bfloat16),
            pltpu.VMEM((STRIP_ROWS, COLUMNS), jnp.float32),
            pltpu.VMEM((1024, 3 * PATCH), jnp.bfloat16),
            pltpu.VMEM((LANES, ACROSS_COUNT * LANES), jnp.bfloat16),
            pltpu.VMEM((LANES, 2 * LANES), jnp.float32),
            pltpu.SemaphoreType.DMA((3,)),
        ],
        compiler_params=pltpu.CompilerParams(vmem_limit_bytes=28 << 20),
        name="stamps",
    )(
        scalars,
        stamp_rows[0],
        stamp_cols[0],
        *[kept(part) for part in parts_a + parts_b],
        picture,
        variance[0],
        pltpu.with_memory_space_constraint(jnp.asarray(stamp_down()), HBM),
        pltpu.with_memory_space_constraint(jnp.asarray(stamp_across()), HBM),
    )
    total = reduce_strips(gram)
    band = across_band(LANES)
    bands = [
        kept(jnp.asarray(band[:, first : first + degree + 1].reshape(2 * LANES, -1)))
        for first, degree in zip((G0, G1, G2), DEGREES)
    ]
    result = pl.pallas_call(
        model_kernel,
        out_shape=jax.ShapeDtypeStruct((STRIP_ROWS, COLUMNS), jnp.float32),
        in_specs=[smem()] + [vmem()] * 7,
        out_specs=vmem(),
        scratch_shapes=[
            pltpu.VMEM((11, STRIP_ROWS, TILE_COUNT * LANES), jnp.bfloat16),
            pltpu.VMEM((COLUMNS // LANES, SLOTS, LANES), jnp.float32),
            pltpu.VMEM((COLUMNS // LANES, SLOTS, LANES), jnp.float32),
            pltpu.VMEM((SLOTS, STRIP_ROWS, LANES), jnp.float32),
            pltpu.VMEM((SLOTS, 2 * STRIP_ROWS, LANES), jnp.float32),
            pltpu.VMEM((SLOTS, 2 * STRIP_ROWS, LANES), jnp.float32),
        ],
        compiler_params=pltpu.CompilerParams(vmem_limit_bytes=32 << 20),
        name="model",
    )(jnp.stack([row_base] + [row_base * 0] * 4), kept(total), window, kept(jnp.asarray(full_down())), picture, *bands)
    return result[None]


def solution(mesh):
    in_specs = (
        P("exp", "strip", None),
        P("exp", "strip", None),
        P(None, "exp"),
        P("exp"),
        P("exp"),
        P("exp", "strip"),
        P("exp", "strip"),
    )
    out_specs = P("exp", "strip", None)
    return jax.shard_map(shards, mesh=mesh, in_specs=in_specs, out_specs=out_specs, check_vma=False)
```

```python
import itertools

import jax
import jax.numpy as jnp
import ml_dtypes
import numpy as np
from jax import lax
from jax.experimental import pallas as pl
from jax.experimental.pallas import tpu as pltpu
from jax.sharding import PartitionSpec as P

STRIP_ROWS = 128
COLUMNS = 2048
IMAGE_ROWS = 512
STAMP_COUNT = 16
STAMP_SIZE = 32
SPATIAL_TERMS = 6
KERNEL_HALF = 20
UNKNOWNS = 165
RIDGE = 0.001
SIGMAS = (1.0, 2.0, 4.0)
DEGREES = (4, 2, 2)

LANES = 128
SOURCE_COLS = 68
NEED_ROWS = 192
WIDE = 2176
TILE_COUNT = 18
PATCH = 80
WINDOW = 176
CUT_ROWS = 40
PIECE_A = 56
PIECE_B = 48

G0, G1, G2 = 0, 5, 8
TILES = (
    ((G0 + 0, (0, 1, 2, 3, 4)), (G0 + 2, (0, 1, 2))),
    ((G0 + 1, (0, 1, 2, 3)), (G0 + 3, (0, 1)), (G0 + 4, (0,))),
    ((G1 + 0, (5, 6, 7)), (G1 + 1, (5, 6)), (G1 + 2, (5,))),
    ((G2 + 0, (8, 9, 10)), (G2 + 1, (8, 9)), (G2 + 2, (8,))),
)
CONST_SLOT = 15
SCIENCE_SLOT = 22
SLOTS = 32
PADDED = SPATIAL_TERMS * SLOTS
POWERS = ((1, 0), (0, 1), (0, 0), (2, 0), (0, 2), (1, 1))
AT_X, AT_Y, AT_ONE, AT_XX, AT_YY, AT_XY = range(SPATIAL_TERMS)
SCIENCE_LANE = SLOTS * AT_ONE + SCIENCE_SLOT
PACKED_ROWS = 5 * SLOTS


def packed_blocks():
    blocks = {}
    for r, left in enumerate(POWERS[2:]):
        for c, right in enumerate(POWERS[:4]):
            blocks.setdefault((left[0] + right[0], left[1] + right[1]), (r, c))
    blocks[(1, 3)] = (4, 0)
    blocks[(0, 4)] = (4, 1)
    return blocks


def tap_table():
    offsets = np.arange(-KERNEL_HALF, KERNEL_HALF + 1).astype(np.float64)
    entries = []
    for spread, degree in zip(SIGMAS, DEGREES):
        profile = np.exp(-offsets * offsets / (2.0 * spread * spread))
        profile = profile / profile.sum()
        for exponent in range(degree + 1):
            entries.append((offsets / spread) ** exponent * profile)
    table = np.stack(entries)
    table[np.abs(table) < 1.2e-38] = 0.0
    return table.astype(np.float32)


def split_halves(table):
    high = table.astype(ml_dtypes.bfloat16)
    low = (table - high.astype(np.float32)).astype(ml_dtypes.bfloat16)
    return high, low


def down_rows(filters, rows):
    taps = tap_table()
    full = np.zeros((len(filters), rows, PATCH), np.float32)
    for i, f in enumerate(filters):
        if f is not None:
            for r in range(rows):
                full[i, r, r : r + 2 * KERNEL_HALF + 1] = taps[f]
    high, low = split_halves(full)
    return np.concatenate([high, high, low], axis=2)


def stamp_down():
    blocks = []
    for tile in TILES:
        filters = [f for _, down in tile for f in down]
        filters += [None] * (8 - len(filters))
        blocks.append(down_rows(filters, STAMP_SIZE).transpose(1, 0, 2).reshape(-1, 3 * PATCH))
    return np.concatenate(blocks)


def full_down():
    return down_rows(list(range(11)), STAMP_SIZE).reshape(-1, 3 * PATCH)


def across_band(width):
    short = tap_table().astype(ml_dtypes.bfloat16)
    band = np.zeros((2 * LANES, 11, width), ml_dtypes.bfloat16)
    for m in range(11):
        for c in range(width):
            band[c : c + 2 * KERNEL_HALF + 1, m, c] = short[m]
    return band


def stamp_across():
    band = across_band(STAMP_SIZE)[:LANES]
    return np.concatenate([np.tile(band[:, m], (1, 4)) for tile in TILES for m, _ in tile], axis=1)


ACROSS_COUNT = sum(len(tile) for tile in TILES)


def slot_of():
    slots = []
    for t, tile in enumerate(TILES):
        s = 8 * t
        for across, down in tile:
            for f in down:
                slots.append((s, f, across))
                s += 1
    return slots


def pack_kernel(strip_ref, template_ref, piece_ref):
    start = pl.multiple_of(strip_ref[0] * LANES, LANES)
    first = template_ref[:, pl.ds(start, LANES)]
    second = template_ref[:, pl.ds(start + LANES, NEED_ROWS - LANES)]
    half = SOURCE_COLS // 2
    piece_ref[0:PIECE_A, :] = first[:PIECE_A]
    piece_ref[PIECE_A + PIECE_B - 8 :, :] = jnp.zeros((8, LANES), jnp.float32)
    piece_ref[PIECE_A : PIECE_A + half, 0:64] = second[:half]
    piece_ref[PIECE_A : PIECE_A + half, 64:128] = second[half:]
    piece_ref[PIECE_A + half : half + SOURCE_COLS, :] = first[PIECE_A:]


def stamps_kernel(scalars, rows_ref, cols_ref, *refs):
    a_refs = refs[0:4]
    b_refs = refs[4:8]
    science_ref, variance_ref, down_hbm, across_hbm = refs[8:12]
    gram_ref, window_ref = refs[12:14]
    t_one, t_two, w_buf, patches, vert, cut_buf, sci_buf, wt_buf, bases, design, across_buf = refs[14:25]
    variance_buf, down_ref, across_ref, sums, copied = refs[25:]
    copies = (
        pltpu.make_async_copy(down_hbm, down_ref, copied.at[0]),
        pltpu.make_async_copy(across_hbm, across_ref, copied.at[1]),
        pltpu.make_async_copy(variance_ref, variance_buf, copied.at[2]),
    )
    for copy in copies:
        copy.start()
    place, shift_down, shift_side, row_base = scalars[0], scalars[1], scalars[2], scalars[3]
    my_z, my_x, my_y = place // 16, (place // 4) % 4, place % 4
    half = SOURCE_COLS // 2
    def direct(own):
        return (own, (own + 3) % 4, (own + 1) % 4, (own + 2) % 4)

    def doubled(own):
        near = own + 1 - 2 * (own % 2)
        return (own, near, 3 - own, 3 - near)

    for first in range(4):
        for second in range(4):
            for dz in range(2):
                for is_a in (True, False):
                    along_x = direct(my_x)[first] if is_a else doubled(my_x)[second]
                    along_y = doubled(my_y)[second] if is_a else direct(my_y)[first]
                    source = ((my_z + dz) % 2) * 16 + along_x * 4 + along_y
                    base = source * SOURCE_COLS
                    if is_a:
                        t_one[pl.ds(base, PIECE_A), :] = a_refs[first][second, dz]
                    else:
                        rest = b_refs[first][second, dz, 0:half, :]
                        t_two[pl.ds(base, half), :] = rest
                        t_two[pl.ds(base + half, half), :] = pltpu.roll(rest, 64, 1)
                        t_one[pl.ds(base + PIECE_A, SOURCE_COLS - PIECE_A), :] = b_refs[first][
                            second, dz, half : half + SOURCE_COLS - PIECE_A, :
                        ]
    t_one[pl.ds(WIDE, 2 * LANES), :] = jnp.zeros((2 * LANES, LANES), jnp.float32)
    t_two[pl.ds(WIDE, 2 * LANES), :] = jnp.zeros((2 * LANES, LANES), jnp.float32)
    w_buf[:, NEED_ROWS:, :] = jnp.zeros((TILE_COUNT, 8, LANES), jnp.float32)

    @pl.loop(0, TILE_COUNT)
    def _(i):
        w_buf[i, 0:LANES, :] = t_one[pl.ds(shift_side + i * LANES, LANES), :].T
        w_buf[i, LANES:NEED_ROWS, :] = t_two[pl.ds(shift_side + i * LANES, LANES), :].T[
            0 : NEED_ROWS - LANES
        ]
        window_ref[i, :, :] = w_buf[i, pl.ds(shift_down, WINDOW), :]

    lane = lax.broadcasted_iota(jnp.int32, (1, LANES), 1)

    @pl.loop(0, STAMP_COUNT)
    def _(s):
        top, left = rows_ref[s], cols_ref[s]
        tile = left // LANES
        rest = left % LANES
        back = (LANES - rest) % LANES
        low = pltpu.roll(window_ref[tile, pl.ds(top, PATCH), :], back, 1)
        high = pltpu.roll(window_ref[tile + 1, pl.ds(top, PATCH), :], back, 1)
        patch = jnp.where(lane < LANES - rest, low, high)
        patch_high = patch.astype(jnp.bfloat16)
        patch_low = (patch - patch_high.astype(jnp.float32)).astype(jnp.bfloat16)
        here = pl.ds(pl.multiple_of(s * LANES, LANES), LANES)
        patches[0:PATCH, here] = patch_high
        patches[PATCH : 2 * PATCH, here] = patch_low
        patches[2 * PATCH :, here] = patch_high

    for copy in copies:
        copy.wait()
    slot = lax.broadcasted_iota(jnp.int32, (8, LANES), 0)
    for member in range(4):
        own = ((lane >= STAMP_SIZE * member) & (lane < STAMP_SIZE * (member + 1))).astype(jnp.bfloat16)
        for n in range(ACROSS_COUNT):
            here = slice(n * LANES, (n + 1) * LANES)
            across_buf[member * LANES : (member + 1) * LANES, here] = across_ref[:, here] * own

    sums[...] = jnp.zeros_like(sums)

    def add_products(at):
        sums[:, 0 : PADDED - SLOTS] += lax.dot_general(
            design[at, PADDED - LANES :, :],
            design[at, 0 : PADDED - SLOTS, :],
            (((1,), (1,)), ((), ())),
            preferred_element_type=jnp.float32,
        )

    @pl.loop(0, STAMP_COUNT // 4)
    def _(group):
        science = jnp.zeros((STAMP_SIZE, LANES), jnp.float32)
        noise = jnp.ones((STAMP_SIZE, LANES), jnp.float32)
        x_row = jnp.zeros((1, LANES), jnp.float32)
        y_row = jnp.zeros((1, LANES), jnp.float32)
        for member in range(4):
            s = 4 * group + member
            top, left = rows_ref[s], cols_ref[s]
            tile = left // LANES
            tile_start = pl.multiple_of(tile * LANES, LANES)
            next_start = pl.multiple_of(jnp.minimum(tile + 1, COLUMNS // LANES - 1) * LANES, LANES)
            rest = left % LANES
            turn = (LANES + STAMP_SIZE * member - rest) % LANES
            inside = (lane >= STAMP_SIZE * member) & (lane < STAMP_SIZE * (member + 1))
            from_low = lane - STAMP_SIZE * member + rest < LANES
            row_start = pl.multiple_of(jnp.minimum((top // 8) * 8, STRIP_ROWS - CUT_ROWS), 8)
            row_rest = top - row_start
            pieces = []
            for n, ref in enumerate((science_ref, variance_buf)):
                low = pltpu.roll(ref[pl.ds(row_start, CUT_ROWS), pl.ds(tile_start, LANES)], turn, 1)
                high = pltpu.roll(ref[pl.ds(row_start, CUT_ROWS), pl.ds(next_start, LANES)], turn, 1)
                cut_buf[member, n, :, :] = jnp.where(from_low, low, high)
                pieces.append(cut_buf[member, n, pl.ds(row_rest, STAMP_SIZE), :])
            science = jnp.where(inside, pieces[0], science)
            noise = jnp.where(inside, pieces[1], noise)
            col = (left + lane - STAMP_SIZE * member).astype(jnp.float32)
            row = (row_base + top + jnp.zeros_like(lane)).astype(jnp.float32)
            x_row = jnp.where(inside, (2.0 * col + 1.0 - COLUMNS) / COLUMNS, x_row)
            y_row = jnp.where(inside, (2.0 * row + 1.0 - IMAGE_ROWS) / IMAGE_ROWS, y_row)
        sci_buf[...] = science
        wt_buf[...] = lax.rsqrt(noise)
        x = jnp.broadcast_to(x_row, (8, LANES))
        y_first = jnp.broadcast_to(y_row, (8, LANES))
        vert[...] = jnp.dot(
            down_ref[...],
            patches[:, pl.ds(pl.multiple_of(group * 4 * LANES, 4 * LANES), 4 * LANES)],
            preferred_element_type=jnp.float32,
        ).astype(jnp.bfloat16)
        column = 0
        for t, tile in enumerate(TILES):
            out = jnp.dot(
                vert[t * 256 : (t + 1) * 256, :],
                across_buf[:, column : column + len(tile) * LANES],
                preferred_element_type=jnp.float32,
            )
            column += len(tile) * LANES
            out = out.reshape(STAMP_SIZE, 8, len(tile) * LANES)
            value = out[:, :, 0:LANES]
            edge = len(tile[0][1])
            for i in range(1, len(tile)):
                value = jnp.where(slot[None] >= edge, out[:, :, i * LANES : (i + 1) * LANES], value)
                edge += len(tile[i][1])
            if t == CONST_SLOT // 8:
                value = jnp.where(slot[None] == CONST_SLOT % 8, 1.0, value)
            bases[t, :, :, :] = value

        for r in range(STAMP_SIZE):
            science = jnp.broadcast_to(sci_buf[r : r + 1, :], (8, LANES))
            weight = jnp.broadcast_to(wt_buf[r : r + 1, :], (8, LANES))
            tiles = [bases[t, r] for t in range(4)]
            tiles[SCIENCE_SLOT // 8] = jnp.where(
                slot == SCIENCE_SLOT % 8, science, tiles[SCIENCE_SLOT // 8]
            )
            y = y_first + 2.0 * r / IMAGE_ROWS
            tiles = [b * weight for b in tiles]
            terms = (x, y, None, x * x, y * y, x * y)
            for j, term in enumerate(terms):
                values = tiles if term is None else [b * term for b in tiles]
                design[group + 1, j * SLOTS : (j + 1) * SLOTS, r * LANES : (r + 1) * LANES] = jnp.concatenate(
                    values, axis=0
                ).astype(jnp.bfloat16)

    for at in range(1, STAMP_COUNT // 4 + 1):
        add_products(at)
    gram_ref[0:LANES, :] = sums[:, 0:LANES]
    left = sums[LANES - SLOTS :, LANES:]
    right = pltpu.roll(sums[LANES - 2 * SLOTS : LANES - SLOTS, LANES:], SLOTS, 1)
    gram_ref[LANES:, :] = jnp.where(lane < SLOTS, left, right)


def lane_spread(value, index):
    return jnp.take_along_axis(value, jnp.full((8, LANES), index, jnp.int32), axis=1)


def spread_column(tiles, index):
    return [lane_spread(v, index) for v in tiles]


def row_spread(tiles, index):
    return jnp.broadcast_to(tiles[index // 8][index % 8 : index % 8 + 1, :], (8, LANES))


def solve(gram_ref, beside, first_block):
    row_id = lax.broadcasted_iota(jnp.int32, (8, LANES), 0)
    lane_id = lax.broadcasted_iota(jnp.int32, (8, LANES), 1)
    slots = sorted(s for s, _, _ in slot_of())
    pivots = sorted(slots + [CONST_SLOT])
    active = {32 * j + s for j in range(SPATIAL_TERMS) for s in slots}
    active |= {32 * j + CONST_SLOT for j in range(3)}

    def any_of(ids, chosen):
        mask = jnp.zeros(ids.shape, jnp.bool_)
        for c in chosen:
            mask = mask | (ids == c)
        return mask

    lanes_left = any_of(lane_id, sorted(u for u in active if u < LANES) + [SCIENCE_LANE])
    lanes_right = any_of(lane_id, [u - LANES for u in sorted(active) if u >= LANES])
    left, right = [], []
    total = jnp.zeros((8, LANES), jnp.float32)
    diagonals = []
    blocks = packed_blocks()
    packed = [gram_ref[8 * i : 8 * i + 8, :] for i in range(PACKED_ROWS // 8)]

    def gathered(i, columns):
        own = POWERS[i // 4]
        out = None
        for place, column in enumerate(columns):
            row, lane = blocks[(own[0] + POWERS[column][0], own[1] + POWERS[column][1])]
            source = packed[4 * row + i % 4]
            if place != lane:
                source = pltpu.roll(source, (SLOTS * (place - lane)) % LANES, 1)
            out = source if out is None else jnp.where(lane_id >= SLOTS * place, source, out)
        return out

    for i in range(24):
        rows = any_of(row_id, [u - 8 * i for u in sorted(active) if u // 8 == i])
        whole = packed[4 * (i // 4 - 2) + i % 4] if i >= 8 else gathered(i, (0, 1, 2, 3))
        a = jnp.where(rows & lanes_left, whole, 0.0)
        b = jnp.where(rows & lanes_right, gathered(i, (4, 5)), 0.0)
        diagonal = lane_id == (row_id + 8 * i) % LANES
        total = total + jnp.where(diagonal & rows, a if i < 16 else b, 0.0)
        left.append(a)
        right.append(b)
        diagonals.append((diagonal, rows))
    ridge = jnp.sum(total, axis=(0, 1), keepdims=True) * (RIDGE / UNKNOWNS)
    for i, (diagonal, rows) in enumerate(diagonals):
        added = jnp.where(diagonal, jnp.where(rows, ridge, 1.0), 0.0)
        if i < 16:
            left[i] = left[i] + jnp.where(lane_id == SCIENCE_LANE, 0.0, added)
        else:
            right[i] = right[i] + added

    def eliminate(left, right, high):
        left, right = list(left), list(right)
        columns = jnp.concatenate((right if high else left)[4:], axis=0)
        own = [left[:4], right[:4]] if high else [left[:4]]
        lead = len(own) - 1
        pairs = list(zip(pivots[0::2], pivots[1::2]))
        columns_p, columns_q = (spread_column(own[lead], c) for c in pairs[0])
        for step, (p, q) in enumerate(pairs):
            ahead = [(c, spread_column(own[lead], c)) for c in (pairs[step + 1] if step + 1 < len(pairs) else ())]
            pp, pq = row_spread(columns_p, p), row_spread(columns_q, p)
            qp, qq = row_spread(columns_p, q), row_spread(columns_q, q)
            scale = 1.0 / (pp * qq - pq * qp)

            def advance(tiles):
                row_p, row_q = row_spread(tiles, p), row_spread(tiles, q)
                new_p = (qq * row_p - pq * row_q) * scale
                new_q = (pp * row_q - qp * row_p) * scale
                out = []
                for i in range(4):
                    value = tiles[i] - columns_p[i] * new_p - columns_q[i] * new_q
                    if i == p // 8:
                        value = jnp.where(row_id == p % 8, new_p, value)
                    if i == q // 8:
                        value = jnp.where(row_id == q % 8, new_q, value)
                    out.append(value)
                return out

            following = [advance(tiles) for _, tiles in ahead]
            own = [advance(side) for side in own]
            if following:
                columns_p, columns_q = following
        rows = jnp.concatenate([jnp.concatenate(side, axis=0) for side in own], axis=1)
        rows = jnp.concatenate([rows, jnp.zeros((LANES - SLOTS, rows.shape[1]), jnp.float32)], axis=0)
        change = jnp.dot(
            columns, rows, precision=lax.Precision.HIGHEST, preferred_element_type=jnp.float32
        )
        for i in range(20):
            part = change[8 * i : 8 * i + 8]
            left[4 + i] = left[4 + i] - part[:, 0:LANES]
            if high:
                right[4 + i] = right[4 + i] - part[:, LANES:]
        left = left[4:] + own[0]
        if high:
            right = [pltpu.roll(v, LANES - SLOTS, 1) for v in right[4:] + own[1]]
        else:
            left = [pltpu.roll(v, LANES - SLOTS, 1) for v in left]
        return tuple(left), tuple(right)

    left, right = left[16:] + left[:16], right[16:] + right[:16]

    def both_sides(step, carry):
        beside(step)
        return eliminate(carry[0], carry[1], True)

    def left_side(step, carry):
        beside(2 * step + 2)
        beside(2 * step + 3)
        for f in range(3 * step, min(3 * step + 3, 11)):
            first_block(f)
        return eliminate(carry, (), False)[0]

    left, right = lax.fori_loop(0, 2, both_sides, (tuple(left), tuple(right)))
    for step in range(4):
        left = left_side(step, left)
    left = left[8:] + left[:8]
    return [lane_spread(v, SCIENCE_LANE) for v in left]


def model_kernel(row_ref, gram_ref, window_ref, down_ref, science_ref, *refs):
    across_refs = refs[0:3]
    out_ref = refs[3]
    vert_ref, a_buf, b_buf, c_buf, sums = refs[4:9]

    def filter_down(step):
        pair = jnp.minimum(step, TILE_COUNT // 2 - 1)
        columns = pl.ds(pl.multiple_of(pair * 2 * LANES, 2 * LANES), 2 * LANES)
        for block in range(STRIP_ROWS // STAMP_SIZE):
            rows = slice(block * STAMP_SIZE, block * STAMP_SIZE + PATCH)
            piece = jnp.concatenate([window_ref[2 * pair, rows, :], window_ref[2 * pair + 1, rows, :]], axis=1)
            high = piece.astype(jnp.bfloat16)
            low = (piece - high.astype(jnp.float32)).astype(jnp.bfloat16)
            stacked = jnp.concatenate([high, low, high], axis=0)
            out = jnp.dot(down_ref[...], stacked, preferred_element_type=jnp.float32)
            vert_ref[:, block * STAMP_SIZE : (block + 1) * STAMP_SIZE, columns] = out.astype(
                jnp.bfloat16
            ).reshape(11, STAMP_SIZE, 2 * LANES)

    slots = slot_of()
    group_first = (G0, G1, G2)

    solution_tiles = solve(gram_ref, filter_down, lambda f: None)
    lane_id = lax.broadcasted_iota(jnp.int32, (8, LANES), 1)
    row_id = lax.broadcasted_iota(jnp.int32, (8, LANES), 0)
    blocks = COLUMNS // LANES
    quarters = STRIP_ROWS // 8
    base = row_ref[0]
    for i in range(blocks):
        x = (2.0 * (lane_id + i * LANES).astype(jnp.float32) + 1.0 - COLUMNS) / COLUMNS
        for t in range(4):
            c = [solution_tiles[4 * j + t] for j in range(SPATIAL_TERMS)]
            a_buf[i, 8 * t : 8 * t + 8, :] = c[AT_ONE] + x * (c[AT_X] + x * c[AT_XX])
            b_buf[i, 8 * t : 8 * t + 8, :] = c[AT_Y] + x * c[AT_XY]
    def row_position(q):
        return (2.0 * (row_id + 8 * q + base).astype(jnp.float32) + 1.0 - IMAGE_ROWS) / IMAGE_ROWS

    for q in range(quarters):
        y = row_position(q)
        for s, _, _ in slots:
            curve = jnp.broadcast_to(solution_tiles[4 * AT_YY + s // 8][s % 8 : s % 8 + 1, :], (8, LANES))
            c_buf[s, 8 * q : 8 * q + 8, :] = y * curve

    def add_filter(batch, f, first):
        g = 0 if f < 5 else (1 if f < 8 else 2)
        members = [(s, m) for s, ff, m in slots if ff == f]
        start = pl.multiple_of(batch * 4 * LANES, 4 * LANES)
        out = jnp.dot(
            jnp.concatenate(
                [
                    vert_ref[f, :, pl.ds(pl.multiple_of(start + n * LANES, LANES), 2 * LANES)]
                    for n in range(4)
                ],
                axis=0,
            ),
            across_refs[g][:, 0 : len(members) * LANES],
            preferred_element_type=jnp.float32,
        )
        for n in range(4):
            block = 4 * batch + n
            rows = [(a_buf[block, s : s + 1, :], b_buf[block, s : s + 1, :]) for s, _ in members]
            rows = [tuple(jnp.broadcast_to(v, (8, LANES)) for v in row) for row in rows]
            for q in range(quarters):
                total = None
                for (s, m), (flat, slope) in zip(members, rows):
                    k = m - group_first[g]
                    at = STRIP_ROWS * n + 8 * q
                    curve = c_buf[row_ref[1 + n] + s, 8 * q : 8 * q + 8, :]
                    field = flat + row_position(q) * (slope + curve)
                    value = out[at : at + 8, k * LANES : (k + 1) * LANES] * field
                    total = value if total is None else total + value
                here = slice(8 * q, 8 * q + 8)
                sums[n, here, :] = total if first else sums[n, here, :] + total

    @pl.loop(0, blocks // 4)
    def _(batch):
        for f in range(11):
            add_filter(batch, f, f == 0)
        for n in range(4):
            block = 4 * batch + n
            columns = pl.ds(pl.multiple_of(block * LANES, LANES), LANES)
            flat = jnp.broadcast_to(a_buf[block, CONST_SLOT : CONST_SLOT + 1, :], (8, LANES))
            slope = jnp.broadcast_to(b_buf[block, CONST_SLOT : CONST_SLOT + 1, :], (8, LANES))
            for q in range(quarters):
                here = slice(8 * q, 8 * q + 8)
                base = flat + row_position(q) * slope
                out_ref[here, columns] = science_ref[here, columns] - (base + sums[n, here, :])


def place(z, x, y):
    return (z % 2) * 16 + (x % 4) * 4 + y % 4


def shift(dz, dx, dy):
    return [(place(z, x, y), place(z + dz, x + dx, y + dy)) for z in range(2) for x in range(4) for y in range(4)]


def gather_template(piece):
    def move(value, *step):
        return lax.ppermute(value, "exp", shift(*step))

    def paired(value, axis, partner):
        def other(z, x, y):
            return place(z, partner(x), y) if axis == "x" else place(z, x, partner(y))

        pairs = [(place(z, x, y), other(z, x, y)) for z in range(2) for x in range(4) for y in range(4)]
        return lax.ppermute(value, "exp", pairs)

    def doubled(value, axis):
        near = lax.optimization_barrier(jnp.stack([value, paired(value, axis, lambda i: i ^ 1)]))
        far = paired(near, axis, lambda i: 3 - i)
        return lax.optimization_barrier(jnp.concatenate([near, far]))

    along_x = ((0, 1, 0), (0, -1, 0), (0, 2, 0))
    along_y = ((0, 0, 1), (0, 0, -1), (0, 0, 2))
    other = move(piece, 1, 0, 0)
    both = lax.optimization_barrier(jnp.stack([piece, other]))
    part_a = doubled(both[:, :PIECE_A], "y")
    part_b = doubled(both[:, PIECE_A:], "x")
    parts_a = [part_a] + [move(part_a, *s) for s in along_x]
    parts_b = [part_b] + [move(part_b, *s) for s in along_y]
    return parts_a, parts_b


def reduce_strips(value):
    value = value + lax.ppermute(value, "strip", [(0, 1), (1, 0), (2, 3), (3, 2)])
    return value + lax.ppermute(value, "strip", [(0, 2), (2, 0), (1, 3), (3, 1)])


VMEM = pltpu.MemorySpace.VMEM
SMEM = pltpu.MemorySpace.SMEM
HBM = pltpu.MemorySpace.HBM


def kept(value):
    return pltpu.with_memory_space_constraint(value, VMEM)


def vmem():
    return pl.BlockSpec(memory_space=VMEM)


def smem():
    return pl.BlockSpec(memory_space=SMEM)


def shards(science, variance, template, offset_rows, offset_cols, stamp_rows, stamp_cols):
    strip_index = lax.axis_index("strip")
    place = lax.axis_index("exp")
    row_base = (strip_index * STRIP_ROWS).astype(jnp.int32)
    picture = kept(science[0])
    piece = pl.pallas_call(
        pack_kernel,
        out_shape=pltpu.VMEM((PIECE_A + PIECE_B, LANES), jnp.float32),
        in_specs=[smem(), vmem()],
        out_specs=vmem(),
        name="pack",
    )(strip_index.astype(jnp.int32)[None], template.T)
    parts_a, parts_b = gather_template(piece)
    scalars = jnp.stack([place.astype(jnp.int32), offset_rows[0], offset_cols[0], row_base])
    gram, window = pl.pallas_call(
        stamps_kernel,
        out_shape=(
            pltpu.VMEM((PACKED_ROWS, LANES), jnp.float32),
            pltpu.VMEM((TILE_COUNT, WINDOW, LANES), jnp.float32),
        ),
        in_specs=[smem()] * 3 + [vmem()] * 9 + [pl.BlockSpec(memory_space=pl.ANY)] + [pl.BlockSpec(memory_space=HBM)] * 2,
        out_specs=(vmem(), vmem()),
        scratch_shapes=[
            pltpu.VMEM((WIDE + 2 * LANES, LANES), jnp.float32),
            pltpu.VMEM((WIDE + 2 * LANES, LANES), jnp.float32),
            pltpu.VMEM((TILE_COUNT, NEED_ROWS + 8, LANES), jnp.float32),
            pltpu.VMEM((3 * PATCH, STAMP_COUNT * LANES), jnp.bfloat16),
            pltpu.VMEM((1024, 4 * LANES), jnp.bfloat16),
            pltpu.VMEM((4, 2, CUT_ROWS, LANES), jnp.float32),
            pltpu.VMEM((STAMP_SIZE, LANES), jnp.float32),
            pltpu.VMEM((STAMP_SIZE, LANES), jnp.float32),
            pltpu.VMEM((4, STAMP_SIZE, 8, LANES), jnp.float32),
            pltpu.VMEM((STAMP_COUNT // 4 + 1, PADDED, STAMP_SIZE * LANES), jnp.bfloat16),
            pltpu.VMEM((4 * LANES, ACROSS_COUNT * LANES), jnp.bfloat16),
            pltpu.VMEM((STRIP_ROWS, COLUMNS), jnp.float32),
            pltpu.VMEM((1024, 3 * PATCH), jnp.bfloat16),
            pltpu.VMEM((LANES, ACROSS_COUNT * LANES), jnp.bfloat16),
            pltpu.VMEM((LANES, 2 * LANES), jnp.float32),
            pltpu.SemaphoreType.DMA((3,)),
        ],
        compiler_params=pltpu.CompilerParams(vmem_limit_bytes=28 << 20),
        name="stamps",
    )(
        scalars,
        stamp_rows[0],
        stamp_cols[0],
        *[kept(part) for part in parts_a + parts_b],
        picture,
        variance[0],
        pltpu.with_memory_space_constraint(jnp.asarray(stamp_down()), HBM),
        pltpu.with_memory_space_constraint(jnp.asarray(stamp_across()), HBM),
    )
    total = reduce_strips(gram)
    band = across_band(LANES)
    bands = [
        kept(jnp.asarray(band[:, first : first + degree + 1].reshape(2 * LANES, -1)))
        for first, degree in zip((G0, G1, G2), DEGREES)
    ]
    result = pl.pallas_call(
        model_kernel,
        out_shape=jax.ShapeDtypeStruct((STRIP_ROWS, COLUMNS), jnp.float32),
        in_specs=[smem()] + [vmem()] * 7,
        out_specs=vmem(),
        scratch_shapes=[
            pltpu.VMEM((11, STRIP_ROWS, TILE_COUNT * LANES), jnp.bfloat16),
            pltpu.VMEM((COLUMNS // LANES, SLOTS, LANES), jnp.float32),
            pltpu.VMEM((COLUMNS // LANES, SLOTS, LANES), jnp.float32),
            pltpu.VMEM((SLOTS, STRIP_ROWS, LANES), jnp.float32),
            pltpu.VMEM((4, STRIP_ROWS, LANES), jnp.float32),
        ],
        compiler_params=pltpu.CompilerParams(vmem_limit_bytes=32 << 20),
        name="model",
    )(jnp.stack([row_base] + [row_base * 0] * 4), kept(total), window, kept(jnp.asarray(full_down())), picture, *bands)
    return result[None]


def solution(mesh):
    in_specs = (
        P("exp", "strip", None),
        P("exp", "strip", None),
        P(None, "exp"),
        P("exp"),
        P("exp"),
        P("exp", "strip"),
        P("exp", "strip"),
    )
    out_specs = P("exp", "strip", None)
    return jax.shard_map(shards, mesh=mesh, in_specs=in_specs, out_specs=out_specs, check_vma=False)
```
